32 devices in a mesh: req: 8 (over z, y), head: 4 (over x, core).
Axes of the slice: x: 2, y: 2, z: 4, core: 2. Of those that a mesh axis runs over, the one named last changes fastest.
Arguments:
- stream_in: bfloat16 [512, 2560], P('req'), may hold values from -6 to 6
- norm_gain: float32 [2560], replicated, may hold values from 0.25 to 1.75
- gate_weight: bfloat16 [2560, 5120], P(None, 'head'), may hold values from -0.125 to 0.125
- inner_weight: bfloat16 [2560, 5120], P(None, 'head'), may hold values from -0.125 to 0.125
- readwrite_weight: bfloat16 [2560, 256], replicated, may hold values from -0.125 to 0.125
- step_weight: bfloat16 [2560, 80], P(None, 'head'), may hold values from -0.125 to 0.125
- conv_inner: bfloat16 [4, 5120], P(None, 'head'), may hold values from -3 to 3
- conv_readwrite: bfloat16 [4, 256], replicated, may hold values from -3 to 3
- decay_log: float32 [80], P('head'), may hold values from 0 to 2.77
- step_bias: float32 [80], P('head'), may hold values from -4 to -1
- skip_gain: float32 [80], P('head'), may hold values from 0.5 to 1.5
- gate_gain: float32 [5120], P('head'), may hold values from 0.25 to 1.75
- out_weight: bfloat16 [5120, 2560], P('head'), may hold values from -0.078125 to 0.078125
- final_gain: float32 [2560], replicated, may hold values from 0.25 to 1.75
- embedding: bfloat16 [50304, 2560], P(('req', 'head')), may hold values from -0.375 to 0.375
- state_cache: bfloat16 [128, 80, 64, 128], P('req', 'head'), may hold values from -4 to 4
- window_inner: bfloat16 [128, 3, 5120], P('req', None, 'head'), may hold values from -6 to 6
- window_readwrite: bfloat16 [128, 3, 256], P('req'), may hold values from -6 to 6
- source_row: int32 [128], replicated, may hold values from 0 to 127, as said below
- lengths: int32 [128], P('req'), may hold values from 1 to 4, 320 in all
- draft_ids: int32 [512], replicated, may hold values from 0 to 50303
Outputs:
- state_after: bfloat16 [128, 80, 64, 128], P('req', 'head')
- tail_inner: bfloat16 [128, 3, 5120], P('req', None, 'head')
- tail_readwrite: bfloat16 [128, 3, 256], P('req')
- hidden_rms: float32 [512], P(('req', 'head'))
- top_logit: float32 [512], P(('req', 'head'))
- draft_logit: float32 [512], P(('req', 'head'))
The draws below stay inside these ranges and needn't reach their ends.
Inputs may be any that keep to these rules, and one draw needn't show every extreme that they name: `source_row`: a permutation of the requests; of the 16 requests r * 16 to r * 16 + 15, exactly 2 have their stored row in each block of 16 rows. The first lengths[r] slots of request r are live.
All inputs are finite; a program needn't handle non-finite values. No bound on the sum of `lengths` on one device may be relied on, other than what follows from the above.
Results may differ from the reference program's by a relative error of at most 0.01.
Values may be sent and summed in bfloat16 or wider, within the bound.
No kernel may reach another device: no remote copies, remote signals or barrier semaphores. Data moves between devices by JAX's collectives and lax.ppermute only.
A program may use at most 320 MiB of HBM per device.

```python
import math
import jax
import jax.numpy as jnp
import numpy as np
from jax import lax

D = 2560
HEADS = 80
HEAD_DIM = 64
STATE = 128
CONV = 4
VOCAB = 50304
SLOTS = 4
R_DEV = 16
INNER = 5120
REQ = 128
TOKENS = 512


def draw_source_row(key, part):
    blocks = REQ // R_DEV
    everyone = jnp.arange(REQ, dtype=jnp.int32)
    home = everyone // R_DEV
    shuffle_key, order_key = jax.random.split(jax.random.fold_in(key, 11))
    scores = jax.random.permutation(shuffle_key, REQ).astype(jnp.int32)
    rank = jnp.argsort(jnp.argsort(home * REQ + scores)).astype(jnp.int32) - home * R_DEV
    anchor = (rank + home) % blocks
    mixing = jax.random.permutation(order_key, REQ).astype(jnp.int32)
    order = jnp.argsort(anchor * REQ + mixing).astype(jnp.int32)
    return jnp.argsort(order).astype(jnp.int32)


def touch_ends(values, key, least, largest):
    extent = values.shape
    index_at = [jax.random.randint(jax.random.fold_in(key, axis), (), 0, extent[axis]) for axis in range(len(extent))]
    values = values.at[tuple(index_at)].set(least)
    longest = extent.index(max(extent))
    index_at[longest] = (index_at[longest] + 1) % extent[longest]
    return values.at[tuple(index_at)].set(largest)


def shard_levels(own_key, dims, cuts, least, high):
    gain = 1.0
    for axis_at, blocks in cuts:
        steps = jax.random.uniform(jax.random.fold_in(jax.random.fold_in(own_key, 6), axis_at), (blocks,), jnp.float32, least / len(cuts), high / len(cuts))
        gain = gain * jnp.repeat(jnp.exp(steps), dims[axis_at] // blocks).reshape((-1,) + (1,) * (len(dims) - 1 - axis_at))
    return gain


def rank_table(amount, lean):
    weights = [(1 << 20) // math.isqrt(standing ** lean) + 1 for standing in range(1, amount + 1)]
    deviation = 1 + sum(weights) // (1 << 30)
    return np.cumsum(np.array([max(1, weight // deviation) for weight in weights]))


def ranked_ids(own_key, shape, count, skew):
    table = rank_table(count, skew)
    lot = jax.random.randint(jax.random.fold_in(own_key, 1), shape, 0, int(table[count - 1]))
    rank = jnp.searchsorted(jnp.asarray(table, jnp.int32), lot, side="right")
    return jax.random.permutation(jax.random.fold_in(own_key, 2), count)[rank].astype(jnp.int32)


def split_up(count, total, reach, slope):
    portions = [(1 << 20) // math.isqrt(standing ** slope) + 1 for standing in range(2, count + 1)]
    surplus, counts = total - reach - (count - 1), [1] * (count - 1)
    while surplus > 0:
        free = [i for i in range(count - 1) if counts[i] < reach]
        mass, remaining = sum([portions[i] for i in free]), surplus
        for i in free:
            more = min(reach - counts[i], max(1, remaining * portions[i] // mass), surplus)
            counts[i] = counts[i] + more
            surplus = surplus - more
    return np.array([reach] + counts)


def ragged_sizes(own_key, number_of, total, limit, lean):
    if number_of == 2:
        one = jax.random.randint(own_key, (), max(1, total - limit), min(limit, total - 1) + 1)
        return jnp.stack([one, total - one])
    sizes = jnp.asarray(split_up(number_of, total, limit, lean), jnp.int32)
    pairs = (number_of - 1) // 2
    source_of, receiver = sizes[1:1 + 2 * pairs:2], sizes[2:2 + 2 * pairs:2]
    room = jnp.minimum(source_of - 1, limit - receiver)
    passed = jax.random.randint(jax.random.fold_in(own_key, 1), (pairs,), 0, 1 << 20) % (room + 1)
    sizes = sizes.at[1:1 + 2 * pairs:2].set(source_of - passed).at[2:2 + 2 * pairs:2].set(receiver + passed)
    return sizes[jax.random.permutation(jax.random.fold_in(own_key, 2), number_of)]


def gaussian(rng, dims, width, most, cuts=(), kind=jnp.bfloat16):
    result = width * jax.random.normal(rng, dims, jnp.float32)
    if cuts:
        result = result * shard_levels(rng, dims, cuts, -0.22, 0.18)
    return jnp.clip(result, -most, most).astype(kind)


def setup_inputs(seed: int = 0) -> dict:
    key_of = jax.random.split(jax.random.key(seed), 22)
    stream_in = gaussian(key_of[0], (TOKENS, D), 1.0, 6.0, ((0, 8),))
    norm_gain = jnp.clip(1.0 + 0.15 * jax.random.normal(key_of[1], (D,), jnp.float32), 0.25, 1.75)
    gate_weight = gaussian(key_of[2], (D, INNER), D ** -0.5, 0.125, ((1, 4),))
    inner_weight = gaussian(key_of[3], (D, INNER), D ** -0.5, 0.125, ((1, 4),))
    readwrite_weight = gaussian(key_of[4], (D, 2 * STATE), D ** -0.5, 0.125)
    step_weight = gaussian(key_of[5], (D, HEADS), D ** -0.5, 0.125, ((1, 4),))
    conv_inner = gaussian(key_of[6], (CONV, INNER), CONV ** -0.5, 3.0, ((1, 4),))
    conv_readwrite = gaussian(key_of[7], (CONV, 2 * STATE), CONV ** -0.5, 3.0)
    decay_log = jnp.clip(2.77 * jax.random.uniform(key_of[8], (HEADS,), jnp.float32) ** shard_levels(key_of[8], (HEADS,), ((0, 4),), -0.2, 0.2), 0.0, 2.77)
    step_bias = jnp.clip(-4.0 + 3.0 * jax.random.uniform(key_of[9], (HEADS,), jnp.float32) ** shard_levels(key_of[9], (HEADS,), ((0, 4),), -0.2, 0.2), -4.0, -1.0)
    skip_gain = jnp.clip(0.5 + 1.0 * jax.random.uniform(key_of[10], (HEADS,), jnp.float32) ** shard_levels(key_of[10], (HEADS,), ((0, 4),), -0.2, 0.2), 0.5, 1.5)
    gate_gain = jnp.clip(1.0 + 0.15 * jax.random.normal(key_of[11], (INNER,), jnp.float32), 0.25, 1.75)
    out_weight = gaussian(key_of[12], (INNER, D), INNER ** -0.5, 0.078125, ((0, 4),))
    final_gain = jnp.clip(1.0 + 0.15 * jax.random.normal(key_of[13], (D,), jnp.float32), 0.25, 1.75)
    embedding = gaussian(key_of[14], (VOCAB, D), (D // 9) ** -0.5, 0.375, ((0, 32),))
    state_cache = gaussian(key_of[15], (REQ, HEADS, HEAD_DIM, STATE), 0.3, 4.0, ((0, 8), (1, 4)))
    window_inner = gaussian(key_of[16], (REQ, CONV - 1, INNER), 1.0, 6.0, ((0, 8), (2, 4)))
    window_readwrite = gaussian(key_of[17], (REQ, CONV - 1, 2 * STATE), 1.0, 6.0, ((0, 8),))
    source_row = draw_source_row(jax.random.fold_in(key_of[21], 71), 0)
    lengths = ragged_sizes(key_of[19], REQ, 5 * REQ // 2, SLOTS, 2).astype(jnp.int32)
    draft_ids = touch_ends(ranked_ids(key_of[20], (TOKENS,), VOCAB, 2), jax.random.fold_in(key_of[20], 3), 0, VOCAB - 1).astype(jnp.int32)
    return dict(stream_in=stream_in, norm_gain=norm_gain, gate_weight=gate_weight, inner_weight=inner_weight, readwrite_weight=readwrite_weight, step_weight=step_weight, conv_inner=conv_inner, conv_readwrite=conv_readwrite, decay_log=decay_log, step_bias=step_bias, skip_gain=skip_gain, gate_gain=gate_gain, out_weight=out_weight, final_gain=final_gain, embedding=embedding, state_cache=state_cache, window_inner=window_inner, window_readwrite=window_readwrite, source_row=source_row, lengths=lengths, draft_ids=draft_ids)


epsilon = 1e-05
lowest = -1e+30

def rms_of(values):
    return jnp.sqrt(lax.optimization_barrier(jnp.mean(values * values, axis=-1, keepdims=True)) + epsilon)

def conv_silu(window, weight):
    taps = weight.shape[0]
    count = window.shape[1] - taps + 1
    total = jnp.zeros((window.shape[0], count, window.shape[2]), jnp.float32)
    for kernel_tap in range(taps):
        total = total + window[:, kernel_tap:kernel_tap + count].astype(jnp.float32) * weight[kernel_tap].astype(jnp.float32)
    return jax.nn.silu(total).astype(jnp.bfloat16)

def last_rows(window, lengths, keep):
    places = jnp.arange(window.shape[1], dtype=jnp.int32)
    wide = window.astype(jnp.float32)
    picked = []
    for lag_index in range(keep):
        select = (places[None, :] == lengths[:, None] + lag_index).astype(jnp.float32)
        picked.append(lax.optimization_barrier(jnp.sum(select[:, :, None] * wide, axis=1)))
    return jnp.stack(picked, axis=1).astype(jnp.bfloat16)

def run_slots(state, inner, writes, reads, steps, decays, skip_gain):
    outputs = []
    for slot_index in range(inner.shape[1]):
        current = inner[:, slot_index].astype(jnp.float32)
        update = (steps[:, slot_index, :, None] * current)[..., None] * writes[:, slot_index, None, None, :].astype(jnp.float32)
        state = decays[:, slot_index, :, None, None] * state + update
        value = jnp.einsum('rhpn,rn->rhp', state, reads[:, slot_index].astype(jnp.float32), precision=lax.Precision.HIGHEST)
        outputs.append(value + skip_gain[None, :, None] * current)
    return (state, jnp.stack(outputs, axis=1))

def reference(stream_in, norm_gain, gate_weight, inner_weight, readwrite_weight, step_weight, conv_inner, conv_readwrite, decay_log, step_bias, skip_gain, gate_gain, out_weight, final_gain, embedding, state_cache, window_inner, window_readwrite, source_row, lengths, draft_ids):
    stream = stream_in.astype(jnp.float32)
    normed = (stream / rms_of(stream) * norm_gain).astype(jnp.bfloat16)
    gate_val = jnp.dot(normed, gate_weight, preferred_element_type=jnp.float32).astype(jnp.bfloat16)
    inner_raw = jnp.dot(normed, inner_weight, preferred_element_type=jnp.float32).astype(jnp.bfloat16)
    readwrite_raw = jnp.dot(normed, readwrite_weight, preferred_element_type=jnp.float32).astype(jnp.bfloat16)
    step_raw = jnp.dot(normed, step_weight, preferred_element_type=jnp.float32).astype(jnp.bfloat16)
    old_state = jnp.take(state_cache, source_row, axis=0)
    old_inner = jnp.take(window_inner, source_row, axis=0)
    old_readwrite = jnp.take(window_readwrite, source_row, axis=0)
    full_inner = jnp.concatenate([old_inner, inner_raw.reshape(REQ, SLOTS, INNER)], axis=1)
    full_readwrite = jnp.concatenate([old_readwrite, readwrite_raw.reshape(REQ, SLOTS, 2 * STATE)], axis=1)
    inner_conv = conv_silu(full_inner, conv_inner)
    readwrite_conv = conv_silu(full_readwrite, conv_readwrite)
    tail_inner = last_rows(full_inner, lengths, CONV - 1)
    tail_readwrite = last_rows(full_readwrite, lengths, CONV - 1)
    live = (jnp.arange(SLOTS, dtype=jnp.int32)[None, :] < lengths[:, None]).astype(jnp.float32)
    steps = jax.nn.softplus(step_raw.astype(jnp.float32).reshape(REQ, SLOTS, HEADS) + step_bias) * live[:, :, None]
    decays = jnp.exp(-jnp.exp(decay_log) * steps)
    blocks = REQ // R_DEV

    def one_block(pieces):
        state, inner, writes, reads, block_steps, block_decays = pieces
        final_state, values = run_slots(state.astype(jnp.float32), inner, writes, reads, block_steps, block_decays, skip_gain)
        return (final_state.astype(jnp.bfloat16), values)
    state_after, slot_out = lax.map(one_block, (old_state.reshape(blocks, R_DEV, HEADS, HEAD_DIM, STATE), inner_conv.reshape(blocks, R_DEV, SLOTS, HEADS, HEAD_DIM), readwrite_conv[..., :STATE].reshape(blocks, R_DEV, SLOTS, STATE), readwrite_conv[..., STATE:].reshape(blocks, R_DEV, SLOTS, STATE), steps.reshape(blocks, R_DEV, SLOTS, HEADS), decays.reshape(blocks, R_DEV, SLOTS, HEADS)))
    state_after = state_after.reshape(REQ, HEADS, HEAD_DIM, STATE)
    slot_values = slot_out.reshape(TOKENS, INNER)
    gated = slot_values * jax.nn.silu(gate_val.astype(jnp.float32))
    gated_normed = (gated / rms_of(gated) * gate_gain).astype(jnp.bfloat16)
    mixed = jnp.dot(gated_normed, out_weight, preferred_element_type=jnp.float32)
    residual = stream + mixed
    scale = rms_of(residual)
    final = (residual / scale * final_gain).astype(jnp.bfloat16)
    live_tokens = live.reshape(TOKENS) > 0.5
    row_block = R_DEV * SLOTS
    vocab_ids = jnp.arange(VOCAB, dtype=jnp.int32)

    def logit_block(pieces):
        rows, token_ids = pieces
        logits = lax.dot_general(rows, embedding, (((1,), (1,)), ((), ())), preferred_element_type=jnp.float32)
        picked = lax.optimization_barrier(jnp.max(jnp.where(vocab_ids[None, :] == token_ids[:, None], logits, lowest), axis=1))
        return (lax.optimization_barrier(jnp.max(logits, axis=1)), picked)
    tops, picks = lax.map(logit_block, (final.reshape(TOKENS // row_block, row_block, D), draft_ids.reshape(TOKENS // row_block, row_block)))
    hidden_rms = jnp.where(live_tokens, scale[:, 0], 0.0)
    top_logit = jnp.where(live_tokens, tops.reshape(TOKENS), 0.0)
    draft_logit = jnp.where(live_tokens, picks.reshape(TOKENS), 0.0)
    return (state_after, tail_inner, tail_readwrite, hidden_rms, top_logit, draft_logit)
```

```python
import functools

import jax
import jax.numpy as jnp
from jax import lax
from jax.experimental import pallas as pl
from jax.experimental.pallas import tpu as pltpu
from jax.sharding import PartitionSpec as P

epsilon = 1e-05
lowest = -1e30
f32 = jnp.float32
bf16 = jnp.bfloat16
i32 = jnp.int32
ANY = pl.BlockSpec(memory_space=pl.ANY)


def rms_of(values):
    return jnp.sqrt(jnp.mean(values * values, axis=-1, keepdims=True) + epsilon)


def send_body(req_dev, source, state, inner, readwrite, state_out, inner_out, readwrite_out, sems):
    me = lax.axis_index("req")
    arrays = ((state, state_out), (inner, inner_out), (readwrite, readwrite_out))

    def visit(request, slot):
        row = source[request]
        mine = lax.div(row, req_dev) == me

        @pl.when(mine)
        def _():
            for index, (held, sent) in enumerate(arrays):
                pltpu.make_async_copy(
                    held.at[lax.rem(row, req_dev)], sent.at[slot], sems.at[index, slot]
                ).start()

        return slot + mine.astype(i32)

    lax.fori_loop(0, source.shape[0], visit, jnp.int32(0))
    for slot in range(req_dev):
        for index, (held, sent) in enumerate(arrays):
            pltpu.make_async_copy(held.at[0], sent.at[slot], sems.at[index, slot]).wait()


def send_rows(source_row, state, inner, readwrite):
    req_dev = state.shape[0]
    return pl.pallas_call(
        functools.partial(send_body, req_dev),
        grid_spec=pltpu.PrefetchScalarGridSpec(
            num_scalar_prefetch=1,
            grid=(),
            in_specs=[ANY] * 3,
            out_specs=[ANY] * 3,
            scratch_shapes=[pltpu.SemaphoreType.DMA((3, req_dev))],
        ),
        out_shape=[jax.ShapeDtypeStruct(a.shape, a.dtype) for a in (state, inner, readwrite)],
        name="send_rows",
    )(source_row, state, inner, readwrite)


def read_body(home_row, state, reads, out):
    out[0] = lax.dot_general(
        reads[0], state[0], (((1,), (1,)), ((), ())), preferred_element_type=f32
    )


def read_states(home_row, state, reads):
    req_dev, slots, state_dim = reads.shape
    width = state.shape[1]
    return pl.pallas_call(
        read_body,
        grid_spec=pltpu.PrefetchScalarGridSpec(
            num_scalar_prefetch=1,
            grid=(req_dev,),
            in_specs=[
                pl.BlockSpec((1, width, state_dim), lambda k, rows: (rows[k], 0, 0)),
                pl.BlockSpec((1, slots, state_dim), lambda k, rows: (k, 0, 0)),
            ],
            out_specs=pl.BlockSpec((1, slots, width), lambda k, rows: (k, 0, 0)),
        ),
        out_shape=jax.ShapeDtypeStruct((req_dev, slots, width), f32),
        name="read_states",
    )(home_row, state, reads)


def update_body(heads, place, keep, state, weighted, writes, out):
    request = pl.program_id(0)
    added = lax.dot_general(
        weighted[0], writes[0], (((0,), (0,)), ((), ())), preferred_element_type=f32
    )
    width = added.shape[0] // heads
    for head in range(heads):
        rows = slice(head * width, (head + 1) * width)
        out[0, rows] = (
            state[0, rows].astype(f32) * keep[request, head] + added[rows]
        ).astype(bf16)


def update_states(place, keep, arrived, weighted, writes):
    req_dev, width, state_dim = arrived.shape
    terms = weighted.shape[1]
    return pl.pallas_call(
        functools.partial(update_body, keep.shape[1]),
        grid_spec=pltpu.PrefetchScalarGridSpec(
            num_scalar_prefetch=2,
            grid=(req_dev,),
            in_specs=[
                pl.BlockSpec((1, width, state_dim), lambda q, place, keep: (place[q], 0, 0)),
                pl.BlockSpec((1, terms, width), lambda q, place, keep: (q, 0, 0)),
                pl.BlockSpec((1, terms, state_dim), lambda q, place, keep: (q, 0, 0)),
            ],
            out_specs=pl.BlockSpec((1, width, state_dim), lambda q, place, keep: (q, 0, 0)),
        ),
        out_shape=jax.ShapeDtypeStruct(arrived.shape, bf16),
        name="update_states",
    )(place, keep, arrived, weighted, writes)


def conv_silu(window, weight):
    taps = weight.shape[0]
    count = window.shape[1] - taps + 1
    total = jnp.zeros((window.shape[0], count, window.shape[2]), f32)
    for tap in range(taps):
        total = total + window[:, tap : tap + count].astype(f32) * weight[tap].astype(f32)
    return jax.nn.silu(total).astype(bf16)


def last_rows(window, lengths, keep):
    places = jnp.arange(window.shape[1], dtype=i32)
    wide = window.astype(f32)
    picked = []
    for lag in range(keep):
        select = (places[None, :] == lengths[:, None] + lag).astype(f32)
        picked.append(jnp.sum(select[:, :, None] * wide, axis=1))
    return jnp.stack(picked, axis=1).astype(bf16)


def on_device(
    stream_in,
    norm_gain,
    gate_weight,
    inner_weight,
    readwrite_weight,
    step_weight,
    conv_inner,
    conv_readwrite,
    decay_log,
    step_bias,
    skip_gain,
    gate_gain,
    out_weight,
    final_gain,
    embedding,
    state_cache,
    window_inner,
    window_readwrite,
    source_row,
    lengths,
    draft_ids,
):
    n_req = lax.axis_size("req")
    n_head = lax.axis_size("head")
    req_index = lax.axis_index("req")
    head_index = lax.axis_index("head")
    rows_dev, model = stream_in.shape
    req_dev = lengths.shape[0]
    slots = rows_dev // req_dev
    all_req = source_row.shape[0]
    heads_dev, head_width, state_dim = state_cache.shape[1:]
    inner_dev = inner_weight.shape[1]
    vocab_dev = embedding.shape[0]
    share = rows_dev // n_head
    taps = conv_inner.shape[0]

    states = state_cache.reshape(req_dev, inner_dev, state_dim)
    leaving, leaving_inner, leaving_readwrite = send_rows(
        source_row, states, window_inner, window_readwrite
    )

    request = jnp.arange(all_req, dtype=i32)
    home = source_row // req_dev
    before = (home[None, :] == home[:, None]) & (request[None, :] < request[:, None])
    place = home * req_dev + jnp.sum(before.astype(i32), axis=1)
    at_home = place[None, :] == (req_index * req_dev + jnp.arange(req_dev, dtype=i32))[:, None]
    home_row = jnp.sum(jnp.where(at_home, (source_row % req_dev)[None, :], 0), axis=1)
    my_home = lax.dynamic_slice_in_dim(home, req_index * req_dev, req_dev)
    mine = jnp.arange(req_dev, dtype=i32)
    ahead = (my_home[None, :] < my_home[:, None]) | (
        (my_home[None, :] == my_home[:, None]) & (mine[None, :] < mine[:, None])
    )
    arrival = jnp.sum(ahead.astype(i32), axis=1)

    row = jnp.arange(rows_dev, dtype=i32)
    goes_to = jnp.repeat(arrival, slots) * slots + row % slots
    choose = (goes_to[None, :] == row[:, None]).astype(bf16)
    outgoing = jnp.dot(choose, stream_in, preferred_element_type=f32).astype(bf16)
    home_stream = lax.all_to_all(outgoing, "req", split_axis=0, concat_axis=0, tiled=True)
    got_inner = lax.all_to_all(leaving_inner, "req", split_axis=0, concat_axis=0, tiled=True)
    got_readwrite = lax.all_to_all(
        leaving_readwrite, "req", split_axis=0, concat_axis=0, tiled=True
    )
    arrived = lax.all_to_all(leaving, "req", split_axis=0, concat_axis=0, tiled=True)

    def project(stream):
        stream = stream.astype(f32)
        normed = (stream / rms_of(stream) * norm_gain).astype(bf16)
        inner = jnp.dot(normed, inner_weight, preferred_element_type=f32).astype(bf16)
        readwrite = jnp.dot(normed, readwrite_weight, preferred_element_type=f32).astype(bf16)
        step_raw = jnp.dot(normed, step_weight, preferred_element_type=f32).astype(bf16)
        return normed, inner, readwrite, step_raw

    def windows(inner, readwrite, old_inner, old_readwrite):
        full_inner = jnp.concatenate([old_inner, inner.reshape(req_dev, slots, inner_dev)], axis=1)
        full_readwrite = jnp.concatenate(
            [old_readwrite, readwrite.reshape(req_dev, slots, 2 * state_dim)], axis=1
        )
        return full_inner, full_readwrite

    def step_sizes(step_raw, live):
        raw = step_raw.astype(f32).reshape(req_dev, slots, heads_dev)
        steps = jax.nn.softplus(raw + step_bias) * live[:, :, None]
        return steps, jnp.exp(-jnp.exp(decay_log) * steps)

    spread = (
        jnp.arange(inner_dev, dtype=i32)[None, :] // head_width
        == jnp.arange(heads_dev, dtype=i32)[:, None]
    ).astype(f32)

    def expand(values):
        return jnp.dot(values, spread, precision=lax.Precision.HIGHEST)

    normed, inner, readwrite, step_raw = project(home_stream)
    gate = jnp.dot(normed, gate_weight, preferred_element_type=f32).astype(bf16)
    full_inner, full_readwrite = windows(inner, readwrite, leaving_inner, leaving_readwrite)
    conv_x = conv_silu(full_inner, conv_inner).astype(f32)
    conv_rw = conv_silu(full_readwrite, conv_readwrite)
    writes, reads = conv_rw[..., :state_dim], conv_rw[..., state_dim:]
    steps, decays = step_sizes(step_raw, jnp.ones((req_dev, slots), f32))
    from_state = read_states(home_row, states, reads)
    matches = jnp.einsum("rsn,rjn->rsj", reads, writes, preferred_element_type=f32)
    tables = []
    carried = None
    terms = []
    for slot in range(slots):
        decay = decays[:, slot]
        carried = decay if slot == 0 else carried * decay
        terms = [term * decay for term in terms] + [steps[:, slot]]
        tables.append(carried)
        for index, term in enumerate(terms):
            factor = term * matches[:, slot, index][:, None]
            if index == slot:
                factor = factor + skip_gain[None, :]
            tables.append(factor)
    wide = expand(jnp.concatenate(tables, axis=0)).reshape(len(tables), req_dev, inner_dev)
    outputs = []
    at = 0
    for slot in range(slots):
        value = wide[at] * from_state[:, slot]
        for index in range(slot + 1):
            value = value + wide[at + 1 + index] * conv_x[:, index]
        outputs.append(value)
        at += slot + 2
    slot_values = jnp.stack(outputs, axis=1).reshape(rows_dev, inner_dev)
    gated = slot_values * jax.nn.silu(gate.astype(f32))
    squares = jnp.sum(gated * gated, axis=1, keepdims=True)
    partial = jnp.dot(
        (gated * gate_gain).astype(bf16), out_weight, preferred_element_type=f32
    )
    packed = jnp.concatenate([partial, jnp.broadcast_to(squares, (rows_dev, 128))], axis=1)
    parts = lax.all_to_all(
        packed.reshape(n_head, share, model + 128), "head", split_axis=0, concat_axis=0, tiled=True
    )
    summed = jnp.sum(parts, axis=0)
    mixed = summed[:, :model] / jnp.sqrt(
        summed[:, model : model + 1] / (inner_dev * n_head) + epsilon
    )
    my_stream = lax.dynamic_slice_in_dim(home_stream, head_index * share, share).astype(f32)
    residual = my_stream + mixed
    scale = rms_of(residual)
    final = (residual / scale * final_gain).astype(bf16)

    tokens = n_req * rows_dev
    everyone = lax.all_gather(final, ("req", "head"), axis=0, tiled=True)
    ids = draft_ids.reshape(all_req, slots)
    chosen = place[None, :] == request[:, None]
    ids_at_home = jnp.sum(jnp.where(chosen[:, :, None], ids[None, :, :], 0), axis=1).reshape(tokens)
    logits = lax.dot_general(
        everyone, embedding, (((1,), (1,)), ((), ())), preferred_element_type=f32
    )
    first_id = (req_index * n_head + head_index) * vocab_dev
    vocab_id = first_id + jnp.arange(vocab_dev, dtype=i32)
    matched = jnp.where(ids_at_home[:, None] == vocab_id[None, :], logits, lowest)
    top = jnp.max(logits, axis=1)
    draft = jnp.max(matched, axis=1)
    first_row = req_index * rows_dev + head_index * share
    scales = lax.dynamic_update_slice_in_dim(
        jnp.full((tokens,), lowest, f32), scale[:, 0], first_row, axis=0
    )
    found = lax.pmax(jnp.stack([top, draft, scales]), ("req", "head"))
    my_req = share // slots
    first_req = req_index * req_dev + head_index * my_req
    my_place = lax.dynamic_slice_in_dim(place, first_req, my_req)
    pick = (my_place[:, None] == request[None, :])[None, :, :, None]
    by_request = found.reshape(3, 1, all_req, slots)
    own = jnp.max(jnp.where(pick, by_request, lowest), axis=2)
    my_lengths = lax.dynamic_slice_in_dim(lengths, head_index * my_req, my_req)
    live = jnp.arange(slots, dtype=i32)[None, :] < my_lengths[:, None]
    own = jnp.where(live[None], own, 0.0).reshape(3, share)

    _, inner_own, readwrite_own, step_own = project(stream_in)
    old_inner = jnp.take(got_inner, arrival, axis=0)
    old_readwrite = jnp.take(got_readwrite, arrival, axis=0)
    full_inner, full_readwrite = windows(inner_own, readwrite_own, old_inner, old_readwrite)
    tail_inner = last_rows(full_inner, lengths, taps - 1)
    tail_readwrite = last_rows(full_readwrite, lengths, taps - 1)
    conv_x = conv_silu(full_inner, conv_inner).astype(f32)
    writes = conv_silu(full_readwrite, conv_readwrite)[..., :state_dim]
    live = (jnp.arange(slots, dtype=i32)[None, :] < lengths[:, None]).astype(f32)
    steps, decays = step_sizes(step_own, live)
    keep = jnp.ones((req_dev, heads_dev), f32)
    terms = []
    for slot in reversed(range(slots)):
        terms.append(keep * steps[:, slot])
        keep = keep * decays[:, slot]
    terms = jnp.stack(terms[::-1], axis=1).reshape(rows_dev, heads_dev)
    weighted = expand(terms).reshape(req_dev, slots, inner_dev) * conv_x
    high = weighted.astype(bf16)
    low = (weighted - high.astype(f32)).astype(bf16)
    weighted = jnp.concatenate([high, low], axis=1)
    writes = jnp.concatenate([writes, writes], axis=1)

    arrived, weighted, writes, keep, own = lax.optimization_barrier(
        (arrived, weighted, writes, keep, own)
    )
    state_after = update_states(arrival, keep, arrived, weighted, writes).reshape(state_cache.shape)
    top_logit, draft_logit, hidden_rms = own
    return (state_after, tail_inner, tail_readwrite, hidden_rms, top_logit, draft_logit)


def solution(mesh):
    in_specs = (
        P("req", None),
        P(),
        P(None, "head"),
        P(None, "head"),
        P(),
        P(None, "head"),
        P(None, "head"),
        P(),
        P("head"),
        P("head"),
        P("head"),
        P("head"),
        P("head", None),
        P(),
        P(("req", "head"), None),
        P("req", "head", None, None),
        P("req", None, "head"),
        P("req", None, None),
        P(),
        P("req"),
        P(),
    )
    out_specs = (
        P("req", "head", None, None),
        P("req", None, "head"),
        P("req", None, None),
        P(("req", "head")),
        P(("req", "head")),
        P(("req", "head")),
    )
    return jax.shard_map(
        on_device, mesh=mesh, in_specs=in_specs, out_specs=out_specs, check_vma=False
    )
```

```python
import functools

import jax
import jax.numpy as jnp
from jax import lax
from jax.experimental import pallas as pl
from jax.experimental.pallas import tpu as pltpu
from jax.sharding import PartitionSpec as P

epsilon = 1e-05
lowest = -1e30
f32 = jnp.float32
bf16 = jnp.bfloat16
i32 = jnp.int32
ANY = pl.BlockSpec(memory_space=pl.ANY)


def rms_of(values):
    return jnp.sqrt(jnp.mean(values * values, axis=-1, keepdims=True) + epsilon)


def pieces_body(where, size, rows, start, held, *refs):
    outs, (buffer, arrive, leave) = refs[:-3], refs[-3:]
    steps = [
        (distance, k, piece, order * size + k)
        for piece, distances in enumerate(where)
        for order, distance in enumerate(distances)
        for k in range(size)
    ]

    def read(index):
        distance, k = steps[index][:2]
        return pltpu.make_async_copy(
            held.at[rows[start[distance] + k]], buffer.at[index], arrive.at[index]
        )

    def write(index):
        piece, at = steps[index][2:]
        return pltpu.make_async_copy(buffer.at[index], outs[piece].at[at], leave.at[index])

    for index in range(len(steps)):
        read(index).start()
    for index in range(len(steps)):
        read(index).wait()
        write(index).start()
    for index in range(len(steps)):
        write(index).wait()


def take_pieces(rows, start, held, where, size):
    width, depth = held.shape[1:]
    count = size * sum(len(distances) for distances in where)
    return pl.pallas_call(
        functools.partial(pieces_body, tuple(where), size),
        grid_spec=pltpu.PrefetchScalarGridSpec(
            num_scalar_prefetch=2,
            grid=(),
            in_specs=[ANY],
            out_specs=[ANY] * len(where),
            scratch_shapes=[
                pltpu.VMEM((count, width, depth), held.dtype),
                pltpu.SemaphoreType.DMA((count,)),
                pltpu.SemaphoreType.DMA((count,)),
            ],
        ),
        out_shape=[
            jax.ShapeDtypeStruct((size * len(distances), width, depth), held.dtype)
            for distances in where
        ],
        cost_estimate=pl.CostEstimate(flops=1, bytes_accessed=1, transcendentals=0),
        name="take_pieces",
    )(rows, start, held)


def softplus(values):
    return jnp.maximum(values, 0.0) + jnp.log1p(jnp.exp(-jnp.abs(values)))


def silu(values):
    return values / (1.0 + jnp.exp(-values))


def home_body(
    sizes,
    order,
    tokens,
    norm_gain,
    old_inner,
    old_readwrite,
    conv_inner,
    conv_readwrite,
    heads,
    head_values,
    gate_gain,
    weights_inner,
    weights_readwrite,
    weights_step,
    weights_gate,
    weights_out,
    state,
    packed_out,
    partial_out,
    squares_out,
    stream_out,
    inner_held,
    readwrite_held,
    step_held,
    gate_held,
    out_held,
    state_held,
    normed,
    sums,
    sems,
    state_sems,
):
    requests, slots, state_dim, taps, chunks = sizes
    rows = requests * slots
    lag = taps - 1

    def parts(source, held, at):
        depth = source.shape[0] // chunks
        return [
            pltpu.make_async_copy(
                source.at[pl.ds(c * depth, depth)],
                held.at[pl.ds(c * depth, depth)],
                sems.at[at * chunks + c],
            )
            for c in range(chunks)
        ]

    inner_parts = parts(weights_inner, inner_held, 0)
    gate_parts = parts(weights_gate, gate_held, 1)
    out_parts = parts(weights_out, out_held, 2)
    small = [
        pltpu.make_async_copy(weights_readwrite, readwrite_held, sems.at[3 * chunks]),
        pltpu.make_async_copy(weights_step, step_held, sems.at[3 * chunks + 1]),
    ]
    states = [
        pltpu.make_async_copy(state.at[order[k]], state_held.at[k], state_sems.at[k])
        for k in range(requests)
    ]
    for copy in small + inner_parts + states + gate_parts + out_parts:
        copy.start()

    into = lax.broadcasted_iota(i32, (rows, rows), 0)
    origin = lax.broadcasted_iota(i32, (rows, rows), 1)
    by_slot = (origin == lax.rem(into, requests) * slots + lax.div(into, requests)).astype(bf16)
    stream_bf = jnp.dot(by_slot, tokens[...], preferred_element_type=f32)
    stream_out[...] = stream_bf.astype(bf16)
    scale = jnp.sqrt(jnp.mean(stream_bf * stream_bf, axis=1, keepdims=True) + epsilon)
    normed[...] = (stream_bf / scale * norm_gain[...]).astype(bf16)

    def project(held, copies):
        total = None
        depth = held.shape[0] // len(copies)
        for c, copy in enumerate(copies):
            copy.wait()
            span = pl.ds(c * depth, depth)
            part = jnp.dot(normed[:, span], held[span], preferred_element_type=f32)
            total = part if total is None else total + part
        return total.astype(bf16)

    readwrite = project(readwrite_held, small[:1])
    step_raw = project(step_held, small[1:])
    inner = project(inner_held, inner_parts)

    def of(values, slot):
        return values[slot * requests : (slot + 1) * requests]

    def convolve(old, new, weight):
        window = [old[j].astype(f32) for j in range(lag)]
        window = window + [of(new, slot).astype(f32) for slot in range(slots)]
        outs = []
        for slot in range(slots):
            total = None
            for tap in range(taps):
                part = window[slot + tap] * weight[tap : tap + 1].astype(f32)
                total = part if total is None else total + part
            outs.append(silu(total).astype(bf16))
        return outs

    x = convolve(old_inner, inner, conv_inner[...])
    vectors = convolve(old_readwrite, readwrite, conv_readwrite[...])
    writes = [v[:, :state_dim].astype(f32) for v in vectors]
    reads = [v[:, state_dim:].astype(f32) for v in vectors]

    bias, decay_rate, skip = (head_values[i : i + 1] for i in range(3))
    wide_step = jnp.dot(step_raw, heads[...], preferred_element_type=f32)
    steps = softplus(wide_step + bias)
    decays = jnp.exp(-decay_rate * steps)

    columns = jnp.concatenate(reads + [jnp.zeros((sums.shape[1] - rows, state_dim), f32)], axis=0).T
    column = lax.rem(lax.broadcasted_iota(i32, columns.shape, 1), requests)
    for k in range(requests):
        own = jnp.where(column == k, columns, 0.0).astype(bf16)
        states[k].wait()
        part = jnp.dot(state_held[k], own, preferred_element_type=f32)
        if k == 0:
            sums[...] = part
        else:
            sums[...] += part
    from_state = sums[...].T

    gate = project(gate_held, gate_parts)
    carried = None
    terms = []
    gated = []
    for slot in range(slots):
        decay, step = of(decays, slot), of(steps, slot)
        current = x[slot].astype(f32)
        carried = decay if carried is None else carried * decay
        terms = [term * decay for term in terms] + [step * current]
        value = carried * of(from_state, slot) + skip * current
        for j, term in enumerate(terms):
            match = jnp.sum(reads[slot] * writes[j], axis=1, keepdims=True)
            value = value + match * term
        gated.append(value * silu(of(gate, slot).astype(f32)))
    gated = jnp.concatenate(gated, axis=0)
    squares = jnp.sum(gated * gated, axis=1, keepdims=True)
    weighted = (gated * gate_gain[...]).astype(bf16)
    depth = weighted.shape[1] // chunks
    total = None
    for c, copy in enumerate(out_parts):
        copy.wait()
        part = jnp.dot(
            weighted[:, c * depth : (c + 1) * depth],
            out_held[pl.ds(c * depth, depth)],
            preferred_element_type=f32,
        )
        total = part if total is None else total + part
    partial_out[...] = total
    wide = jnp.broadcast_to(squares, (rows, 128))
    squares_out[...] = wide
    high = wide.astype(bf16)
    low = (wide - high.astype(f32)).astype(bf16)
    model = total.shape[1]
    packed_out[:, :model] = total.astype(bf16)
    packed_out[:, model : model + 128] = high
    packed_out[:, model + 128 :] = low


def home_tokens(order, tokens, small, big, state, slots, taps):
    rows, model = tokens.shape
    requests, width, state_dim = state.shape
    chunks = 5
    lanes = rows + -rows % 128
    in_vmem = pl.BlockSpec(memory_space=pltpu.VMEM)
    return pl.pallas_call(
        functools.partial(home_body, (requests, slots, state_dim, taps, chunks)),
        grid_spec=pltpu.PrefetchScalarGridSpec(
            num_scalar_prefetch=1,
            grid=(),
            in_specs=[in_vmem] * (1 + len(small)) + [ANY] * (len(big) + 1),
            out_specs=[in_vmem] * 4,
            scratch_shapes=[pltpu.VMEM(w.shape, w.dtype) for w in big]
            + [
                pltpu.VMEM(state.shape, state.dtype),
                pltpu.VMEM((rows, model), bf16),
                pltpu.VMEM((width, lanes), f32),
                pltpu.SemaphoreType.DMA((3 * chunks + 2,)),
                pltpu.SemaphoreType.DMA((requests,)),
            ],
        ),
        out_shape=[
            jax.ShapeDtypeStruct((rows, model + 256), bf16),
            jax.ShapeDtypeStruct((rows, model), f32),
            jax.ShapeDtypeStruct((rows, 128), f32),
            jax.ShapeDtypeStruct((rows, model), bf16),
        ],
        compiler_params=pltpu.CompilerParams(vmem_limit_bytes=48 << 20),
        cost_estimate=pl.CostEstimate(flops=1, bytes_accessed=1, transcendentals=0),
        name="home_tokens",
    )(order, tokens, *small, *big, state)


def update_body(where, size, heads, target, start, keep, weighted, writes, *refs):
    pieces = refs[: len(where)]
    out, before, after, arrive, leave = refs[-5:]
    count = len(where) * size

    def at(index):
        return start[where[index // size]] + index % size

    def read(index):
        return pltpu.make_async_copy(
            pieces[index // size].at[index % size], before.at[index], arrive.at[index]
        )

    def write(index):
        return pltpu.make_async_copy(after.at[index], out.at[target[at(index)]], leave.at[index])

    for index in range(count):
        read(index).start()
    width = weighted.shape[0] // heads
    for index in range(count):
        request = at(index)
        added = jnp.dot(weighted[...], writes[request], preferred_element_type=f32)
        read(index).wait()
        for head in range(heads):
            rows = slice(head * width, (head + 1) * width)
            after[index, rows] = (
                before[index, rows].astype(f32) * keep[request, head] + added[rows]
            ).astype(bf16)
        write(index).start()
    for index in range(count):
        write(index).wait()


def update_pieces(target, start, keep, weighted, writes, where, pieces, whole):
    size, width, state_dim = pieces[0].shape
    req_dev, heads = keep.shape
    count = len(where) * size
    return pl.pallas_call(
        functools.partial(update_body, tuple(where), size, heads),
        grid_spec=pltpu.PrefetchScalarGridSpec(
            num_scalar_prefetch=3,
            grid=(),
            in_specs=[pl.BlockSpec(memory_space=pltpu.VMEM)] * 2
            + [ANY] * (len(where) + len(whole)),
            out_specs=ANY,
            scratch_shapes=[
                pltpu.VMEM((count, width, state_dim), bf16),
                pltpu.VMEM((count, width, state_dim), bf16),
                pltpu.SemaphoreType.DMA((count,)),
                pltpu.SemaphoreType.DMA((count,)),
            ],
        ),
        out_shape=jax.ShapeDtypeStruct((req_dev, width, state_dim), bf16),
        input_output_aliases={5 + len(where): 0} if whole else {},
        compiler_params=pltpu.CompilerParams(vmem_limit_bytes=24 << 20),
        name="update_pieces",
    )(target, start, keep, weighted, writes, *pieces, *whole)


def head_body(vocab, first, ids, final, rows, top, draft):
    step = pl.program_id(0)
    depth = rows.shape[0]
    logits = lax.dot_general(
        rows[...], final[...], (((1,), (1,)), ((), ())), preferred_element_type=f32
    )
    row = step * depth + lax.broadcasted_iota(i32, logits.shape, 0)
    logits = jnp.where(row < vocab, logits, lowest)
    best = jnp.max(logits, axis=0, keepdims=True)
    match = jnp.max(
        jnp.where(row + first[0] == ids[...], logits, lowest), axis=0, keepdims=True
    )

    @pl.when(step == 0)
    def _():
        top[...] = best
        draft[...] = match

    @pl.when(step > 0)
    def _():
        top[...] = jnp.maximum(top[...], best)
        draft[...] = jnp.maximum(draft[...], match)


def head_logits(first, ids, final, embedding):
    vocab, model = embedding.shape
    tokens = final.shape[0]
    depth = 400
    return pl.pallas_call(
        functools.partial(head_body, vocab),
        grid_spec=pltpu.PrefetchScalarGridSpec(
            num_scalar_prefetch=1,
            grid=(pl.cdiv(vocab, depth),),
            in_specs=[
                pl.BlockSpec((1, tokens), lambda i, first: (0, 0)),
                pl.BlockSpec((tokens, model), lambda i, first: (0, 0)),
                pl.BlockSpec((depth, model), lambda i, first: (i, 0)),
            ],
            out_specs=[pl.BlockSpec((1, tokens), lambda i, first: (0, 0))] * 2,
        ),
        out_shape=[jax.ShapeDtypeStruct((1, tokens), f32)] * 2,
        compiler_params=pltpu.CompilerParams(vmem_limit_bytes=24 << 20),
        cost_estimate=pl.CostEstimate(
            flops=2 * vocab * model * tokens,
            bytes_accessed=2 * vocab * model,
            transcendentals=0,
        ),
        name="head_logits",
    )(first, ids, final, embedding)


def on_device(
    stream_in,
    norm_gain,
    gate_weight,
    inner_weight,
    readwrite_weight,
    step_weight,
    conv_inner,
    conv_readwrite,
    decay_log,
    step_bias,
    skip_gain,
    gate_gain,
    out_weight,
    final_gain,
    embedding,
    state_cache,
    window_inner,
    window_readwrite,
    source_row,
    lengths,
    draft_ids,
):
    n_req = lax.axis_size("req")
    n_head = lax.axis_size("head")
    req_index = lax.axis_index("req")
    head_index = lax.axis_index("head")
    rows_dev, model = stream_in.shape
    req_dev = lengths.shape[0]
    slots = rows_dev // req_dev
    all_req = source_row.shape[0]
    heads_dev, head_width, state_dim = state_cache.shape[1:]
    inner_dev = inner_weight.shape[1]
    vocab_dev = embedding.shape[0]
    share = rows_dev // n_head
    taps = conv_inner.shape[0]

    each = req_dev // n_req
    states = state_cache.reshape(req_dev, inner_dev, state_dim)

    def swap(values, axis, mask):
        return lax.ppermute(values, axis, [(i, i ^ mask) for i in range(lax.axis_size(axis))])

    request = jnp.arange(all_req, dtype=i32)
    block = request // req_dev
    home = source_row // req_dev
    before = (
        (home[None, :] == home[:, None])
        & (block[None, :] == block[:, None])
        & (request[None, :] < request[:, None])
    )
    rank = jnp.sum(before.astype(i32), axis=1)
    place = (block ^ home) * each + rank
    listed = jnp.arange(req_dev, dtype=i32)[:, None]
    is_home = (listed == place[None, :]) & (home == req_index)[None, :]
    is_target = (listed == place[None, :]) & (block == req_index)[None, :]
    start = jnp.arange(n_req, dtype=i32) * each
    home_row = jnp.sum(jnp.where(is_home, (source_row % req_dev)[None, :], 0), axis=1)
    target = jnp.sum(jnp.where(is_target, (request % req_dev)[None, :], 0), axis=1)

    mine = jnp.arange(req_dev, dtype=i32)
    to_target = (target[:, None] == mine[None, :]).astype(bf16)
    to_home = (home_row[:, None] == mine[None, :]).astype(bf16)
    row = jnp.arange(rows_dev, dtype=i32)
    source_token = jnp.repeat(target, slots) * slots + row % slots
    tokens_out = jnp.dot(
        (source_token[:, None] == row[None, :]).astype(bf16),
        stream_in,
        preferred_element_type=f32,
    ).astype(bf16)

    def choose(selector, values):
        return jnp.einsum("kr,rjc->jkc", selector, values, preferred_element_type=f32).astype(bf16)

    home_inner = choose(to_home, window_inner)
    home_readwrite = choose(to_home, window_readwrite)
    lag = taps - 1
    packed_inner = home_inner.reshape(lag, n_req, each * inner_dev).transpose(1, 0, 2)
    packed_readwrite = (
        home_readwrite.reshape(lag, n_req, each * 2 * state_dim)
        .transpose(1, 0, 2)
        .reshape(n_req, 1, lag * each * 2 * state_dim)
    )
    letters = jnp.concatenate(
        [
            tokens_out.reshape(n_req, each * slots, model),
            jnp.pad(packed_inner, ((0, 0), (0, 0), (0, model - packed_inner.shape[2]))),
            jnp.pad(packed_readwrite, ((0, 0), (0, 0), (0, model - packed_readwrite.shape[2]))),
        ],
        axis=1,
    )
    outgoing = letters
    pairs = [letters[:2]]
    for mask in range(2, n_req, 2):
        pairs.append(swap(letters[mask : mask + 2], "req", mask))
    direct = [d for d in range(1, n_req) if d > 3] if n_req > 3 else []
    phases = ([n_req - 2], [d for d in direct if d != n_req - 2])
    home_row_a, outgoing = lax.optimization_barrier((home_row, outgoing))
    pair, *leaving_a = take_pieces(
        home_row_a, start, states, [(2, 3)] + [(d,) for d in phases[0]], each
    )
    pairs, pair, leaving_a = lax.optimization_barrier((pairs, pair, leaving_a))
    arrived = {}
    for d, value in zip(phases[0], leaving_a):
        arrived[d] = swap(value, "req", d)
    pair = swap(pair, "req", 2)
    arrived[2] = pair[:each]
    kept = jnp.stack([both[0] for both in pairs])
    passed = swap(jnp.stack([both[1] for both in pairs]), "req", 1)
    letters = jnp.stack([kept, passed], axis=1).reshape(letters.shape)

    home_stream = letters[:, : each * slots].reshape(rows_dev, model)
    got_inner = (
        letters[:, each * slots : each * slots + lag, : each * inner_dev]
        .transpose(1, 0, 2)
        .reshape(lag, req_dev, inner_dev)
    )
    got_readwrite = (
        letters[:, each * slots + lag, : lag * each * 2 * state_dim]
        .reshape(n_req, lag, each * 2 * state_dim)
        .transpose(1, 0, 2)
        .reshape(lag, req_dev, 2 * state_dim)
    )

    def project(stream):
        stream = stream.astype(f32)
        normed = (stream / rms_of(stream) * norm_gain).astype(bf16)
        inner = jnp.dot(normed, inner_weight, preferred_element_type=f32).astype(bf16)
        readwrite = jnp.dot(normed, readwrite_weight, preferred_element_type=f32).astype(bf16)
        step_raw = jnp.dot(normed, step_weight, preferred_element_type=f32).astype(bf16)
        return normed, inner, readwrite, step_raw

    def windows(old, new):
        new = new.reshape(req_dev, slots, new.shape[1])
        return [old[j] for j in range(lag)] + [new[:, s] for s in range(slots)]

    def conv_silu(rows, weight):
        outs = []
        for slot in range(slots):
            total = jnp.zeros(rows[0].shape, f32)
            for tap in range(taps):
                total = total + rows[slot + tap].astype(f32) * weight[tap].astype(f32)
            outs.append(jax.nn.silu(total).astype(bf16))
        return outs

    def step_sizes(step_raw, live):
        raw = step_raw.astype(f32).reshape(req_dev, slots, heads_dev)
        steps = jax.nn.softplus(raw + step_bias) * live[:, :, None]
        return steps, jnp.exp(-jnp.exp(decay_log) * steps)

    spread = (
        jnp.arange(inner_dev, dtype=i32)[None, :] // head_width
        == jnp.arange(heads_dev, dtype=i32)[:, None]
    ).astype(f32)

    def expand(values):
        return jnp.dot(values, spread, precision=lax.Precision.HIGHEST)

    head_values = jnp.repeat(
        jnp.stack([step_bias, jnp.exp(decay_log), skip_gain]), head_width, axis=1
    )
    packed, partial, squares, home_stream = home_tokens(
        home_row,
        home_stream,
        (
            norm_gain[None, :],
            home_inner,
            home_readwrite,
            conv_inner,
            conv_readwrite,
            spread.astype(bf16),
            head_values,
            gate_gain[None, :],
        ),
        (inner_weight, readwrite_weight, step_weight, gate_weight, out_weight),
        states,
        slots,
        taps,
    )

    def rows_of(values, index):
        return lax.dynamic_slice_in_dim(values, index * share, share)

    mixed = rows_of(partial, head_index)
    total = rows_of(squares, head_index)[:, :1]
    for mask in range(1, n_head):
        part = swap(rows_of(packed, head_index ^ mask), "head", mask).astype(f32)
        mixed = mixed + part[:, :model]
        total = total + part[:, model : model + 1] + part[:, model + 128 : model + 129]
    mixed = mixed / jnp.sqrt(total / (inner_dev * n_head) + epsilon)
    residual = rows_of(home_stream, head_index).astype(f32) + mixed
    scale = rms_of(residual)
    final = (residual / scale * final_gain).astype(bf16)

    distance = [0]
    final, home_row_b = lax.optimization_barrier((final, home_row))
    local, neighbour, *leaving_b = take_pieces(
        home_row_b, start, states, [(0,), (1,)] + [(d,) for d in phases[1]], each
    )
    arrived[0] = local
    for d, value in zip(phases[1], leaving_b):
        arrived[d] = swap(value, "req", d)
    everyone = final
    for step, (axis, masks) in enumerate((
        ("req", range(2, n_req, 2)),
        ("req", (1,)),
        ("head", range(2, n_head, 2)),
        ("head", (1,)),
    )):
        if step == 3:
            first_late = phases[1][0]
            everyone, arrived[first_late] = lax.optimization_barrier(
                (everyone, arrived[first_late])
            )
        everyone = jnp.concatenate([everyone] + [swap(everyone, axis, m) for m in masks], axis=0)
        if step == 1:
            passed_on = jnp.concatenate([neighbour, pair[each:]])
            everyone, passed_on = lax.optimization_barrier((everyone, passed_on))
            passed_on = swap(passed_on, "req", 1)
            arrived[1], arrived[3] = passed_on[:each], passed_on[each:]
        unit = n_head if axis == "req" else 1
        distance = distance + [e ^ (m * unit) for m in masks for e in distance]

    tokens = n_req * rows_dev
    my_req = share // slots
    my_device = req_index * n_head + head_index
    local = jnp.arange(slots, dtype=i32)[None, :] * req_dev + place[:, None]
    local = local.reshape(tokens)
    from_device = jnp.repeat(home, slots) * n_head + local // share
    away = (from_device ^ my_device)[:, None] == jnp.array(distance, dtype=i32)[None, :]
    found_at = jnp.sum(
        jnp.where(away, jnp.arange(len(distance), dtype=i32)[None, :], 0), axis=1
    ) * share + local % share
    token = jnp.arange(tokens, dtype=i32)
    pick = found_at[:, None] == token[None, :]
    ids_here = jnp.sum(jnp.where(pick, draft_ids[:, None], 0), axis=0)
    first_row = jnp.full((1,), my_device * vocab_dev, i32)
    top, draft = head_logits(first_row, ids_here[None, :], everyone, embedding)
    held = [1, 3] + phases[1][1:2]
    top, draft, *values = lax.optimization_barrier((top, draft, *(arrived[d] for d in held)))
    arrived.update(zip(held, values))
    scales = jnp.concatenate([scale[:, 0], jnp.full((tokens - share,), lowest, f32)])
    found = jnp.concatenate([top, draft, scales[None, :]])
    found = jnp.max(jnp.where(pick[None], found[:, None, :], lowest), axis=2)
    found = found.reshape(3, n_req, n_head, share)

    def for_head(index):
        return lax.dynamic_index_in_dim(found, index, axis=2, keepdims=False)

    best = for_head(head_index)
    for mask in range(1, n_head):
        best = jnp.maximum(best, swap(for_head(head_index ^ mask), "head", mask))


    def for_req(distance):
        return lax.dynamic_index_in_dim(best, req_index ^ distance, axis=1, keepdims=False)

    far = swap(jnp.stack([for_req(mask ^ 1) for mask in range(0, n_req, 2)]), "req", 1)
    own = jnp.maximum(for_req(0), far[0])
    for mask in range(2, n_req, 2):
        own = jnp.maximum(own, swap(jnp.maximum(for_req(mask), far[mask // 2]), "req", mask))
    my_lengths = lax.dynamic_slice_in_dim(lengths, head_index * my_req, my_req)
    live = jnp.arange(slots, dtype=i32)[None, :] < my_lengths[:, None]
    own = jnp.where(live.reshape(1, share), own, 0.0)

    tokens_out, got_inner, got_readwrite, _ = lax.optimization_barrier(
        (tokens_out, got_inner, got_readwrite, final)
    )
    _, inner, readwrite, step_raw = project(tokens_out)
    rows_inner = windows(got_inner, inner)
    rows_readwrite = windows(got_readwrite, readwrite)
    my_lengths = jnp.sum(jnp.where(to_target > 0, lengths[None, :], 0), axis=1)

    def tails(rows):
        picked = []
        for j in range(lag):
            value = rows[j + 1]
            for length in range(2, slots + 1):
                value = jnp.where(my_lengths[:, None] == length, rows[j + length], value)
            picked.append(value)
        picked = jnp.stack(picked, axis=1)
        return jnp.einsum("kr,kjc->rjc", to_target, picked, preferred_element_type=f32).astype(bf16)

    tail_inner = tails(rows_inner)
    tail_readwrite = tails(rows_readwrite)
    conv_x = conv_silu(rows_inner, conv_inner)
    writes = jnp.stack(conv_silu(rows_readwrite, conv_readwrite), axis=1)[..., :state_dim]
    live = (jnp.arange(slots, dtype=i32)[None, :] < my_lengths[:, None]).astype(f32)
    steps, decays = step_sizes(step_raw, live)
    keep = jnp.ones((req_dev, heads_dev), f32)
    terms = []
    for slot in reversed(range(slots)):
        terms.append(keep * steps[:, slot])
        keep = keep * decays[:, slot]
    wide = expand(jnp.concatenate(terms[::-1], axis=0)).reshape(slots, req_dev, inner_dev)
    weighted = jnp.stack([wide[s] * conv_x[s].astype(f32) for s in range(slots)], axis=1)
    high = weighted.astype(bf16)
    low = (weighted - high.astype(f32)).astype(bf16)
    count = 2 * slots * req_dev
    weighted = jnp.concatenate([high, low], axis=1).reshape(count, inner_dev).T
    writes = jnp.concatenate([writes, writes], axis=1).reshape(1, count, state_dim)
    owner = jnp.arange(count, dtype=i32)[None, :, None] // (2 * slots)
    writes = jnp.where(owner == mine[:, None, None], writes, 0)

    update = functools.partial(update_pieces, target, start, keep, weighted, writes)
    early = [0, 1, 2, 3] + phases[0] + phases[1][:2]
    after = update(early, [arrived[d] for d in early], ())
    late = phases[1][2:]
    after = update(late, [arrived[d] for d in late], (after,))
    state_after = after.reshape(state_cache.shape)
    top_logit, draft_logit, hidden_rms = own
    return (state_after, tail_inner, tail_readwrite, hidden_rms, top_logit, draft_logit)


def solution(mesh):
    in_specs = (
        P("req", None),
        P(),
        P(None, "head"),
        P(None, "head"),
        P(),
        P(None, "head"),
        P(None, "head"),
        P(),
        P("head"),
        P("head"),
        P("head"),
        P("head"),
        P("head", None),
        P(),
        P(("req", "head"), None),
        P("req", "head", None, None),
        P("req", None, "head"),
        P("req", None, None),
        P(),
        P("req"),
        P(),
    )
    out_specs = (
        P("req", "head", None, None),
        P("req", None, "head"),
        P("req", None, None),
        P(("req", "head")),
        P(("req", "head")),
        P(("req", "head")),
    )
    return jax.shard_map(
        on_device, mesh=mesh, in_specs=in_specs, out_specs=out_specs, check_vma=False
    )
```

```python
import functools

import jax
import jax.numpy as jnp
from jax import lax
from jax.experimental import pallas as pl
from jax.experimental.pallas import tpu as pltpu
from jax.sharding import PartitionSpec as P

epsilon = 1e-05
lowest = -1e30
f32 = jnp.float32
bf16 = jnp.bfloat16
i32 = jnp.int32
ANY = pl.BlockSpec(memory_space=pl.ANY)


def rms_of(values):
    return jnp.sqrt(jnp.mean(values * values, axis=-1, keepdims=True) + epsilon)


def pieces_body(where, size, rows, start, held, *refs):
    outs, (buffer, arrive, leave) = refs[:-3], refs[-3:]
    steps = [
        (distance, k, piece, order * size + k)
        for piece, distances in enumerate(where)
        for order, distance in enumerate(distances)
        for k in range(size)
    ]

    def read(index):
        distance, k = steps[index][:2]
        return pltpu.make_async_copy(
            held.at[rows[start[distance] + k]], buffer.at[index], arrive.at[index]
        )

    def write(index):
        piece, at = steps[index][2:]
        return pltpu.make_async_copy(buffer.at[index], outs[piece].at[at], leave.at[index])

    for index in range(len(steps)):
        read(index).start()
    for index in range(len(steps)):
        read(index).wait()
        write(index).start()
    for index in range(len(steps)):
        write(index).wait()


def take_pieces(rows, start, held, where, size):
    width, depth = held.shape[1:]
    count = size * sum(len(distances) for distances in where)
    return pl.pallas_call(
        functools.partial(pieces_body, tuple(where), size),
        grid_spec=pltpu.PrefetchScalarGridSpec(
            num_scalar_prefetch=2,
            grid=(),
            in_specs=[ANY],
            out_specs=[ANY] * len(where),
            scratch_shapes=[
                pltpu.VMEM((count, width, depth), held.dtype),
                pltpu.SemaphoreType.DMA((count,)),
                pltpu.SemaphoreType.DMA((count,)),
            ],
        ),
        out_shape=[
            jax.ShapeDtypeStruct((size * len(distances), width, depth), held.dtype)
            for distances in where
        ],
        cost_estimate=pl.CostEstimate(flops=1, bytes_accessed=1, transcendentals=0),
        name="take_pieces",
    )(rows, start, held)


def softplus(values):
    return jnp.maximum(values, 0.0) + jnp.log1p(jnp.exp(-jnp.abs(values)))


def silu(values):
    return values / (1.0 + jnp.exp(-values))


def home_body(
    sizes,
    order,
    tokens,
    norm_gain,
    old_inner,
    old_readwrite,
    conv_inner,
    conv_readwrite,
    heads,
    head_values,
    gate_gain,
    weights_inner,
    weights_readwrite,
    weights_step,
    weights_gate,
    weights_out,
    state,
    packed_out,
    partial_out,
    squares_out,
    stream_out,
    inner_held,
    readwrite_held,
    step_held,
    gate_held,
    out_held,
    state_held,
    normed,
    sums,
    sems,
    state_sems,
):
    requests, slots, state_dim, taps, chunks = sizes
    rows = requests * slots
    lag = taps - 1

    def parts(source, held, at):
        depth = source.shape[0] // chunks
        return [
            pltpu.make_async_copy(
                source.at[pl.ds(c * depth, depth)],
                held.at[pl.ds(c * depth, depth)],
                sems.at[at * chunks + c],
            )
            for c in range(chunks)
        ]

    inner_parts = parts(weights_inner, inner_held, 0)
    gate_parts = parts(weights_gate, gate_held, 1)
    out_parts = parts(weights_out, out_held, 2)
    small = [
        pltpu.make_async_copy(weights_readwrite, readwrite_held, sems.at[3 * chunks]),
        pltpu.make_async_copy(weights_step, step_held, sems.at[3 * chunks + 1]),
    ]
    states = [
        pltpu.make_async_copy(state.at[order[k]], state_held.at[k], state_sems.at[k])
        for k in range(requests)
    ]
    for copy in small + inner_parts + states + gate_parts + out_parts:
        copy.start()

    into = lax.broadcasted_iota(i32, (rows, rows), 0)
    origin = lax.broadcasted_iota(i32, (rows, rows), 1)
    by_slot = (origin == lax.rem(into, requests) * slots + lax.div(into, requests)).astype(bf16)
    stream_bf = jnp.dot(by_slot, tokens[...], preferred_element_type=f32)
    stream_out[...] = stream_bf.astype(bf16)
    scale = jnp.sqrt(jnp.mean(stream_bf * stream_bf, axis=1, keepdims=True) + epsilon)
    normed[...] = (stream_bf / scale * norm_gain[...]).astype(bf16)

    def project(held, copies):
        total = None
        depth = held.shape[0] // len(copies)
        for c, copy in enumerate(copies):
            copy.wait()
            span = pl.ds(c * depth, depth)
            part = jnp.dot(normed[:, span], held[span], preferred_element_type=f32)
            total = part if total is None else total + part
        return total.astype(bf16)

    readwrite = project(readwrite_held, small[:1])
    step_raw = project(step_held, small[1:])
    inner = project(inner_held, inner_parts)

    def of(values, slot):
        return values[slot * requests : (slot + 1) * requests]

    def convolve(old, new, weight):
        window = [old[j].astype(f32) for j in range(lag)]
        window = window + [of(new, slot).astype(f32) for slot in range(slots)]
        outs = []
        for slot in range(slots):
            total = None
            for tap in range(taps):
                part = window[slot + tap] * weight[tap : tap + 1].astype(f32)
                total = part if total is None else total + part
            outs.append(silu(total).astype(bf16))
        return outs

    x = convolve(old_inner, inner, conv_inner[...])
    vectors = convolve(old_readwrite, readwrite, conv_readwrite[...])
    writes = [v[:, :state_dim].astype(f32) for v in vectors]
    reads = [v[:, state_dim:].astype(f32) for v in vectors]

    bias, decay_rate, skip = (head_values[i : i + 1] for i in range(3))
    wide_step = jnp.dot(step_raw, heads[...], preferred_element_type=f32)
    steps = softplus(wide_step + bias)
    decays = jnp.exp(-decay_rate * steps)

    columns = jnp.concatenate(reads + [jnp.zeros((sums.shape[1] - rows, state_dim), f32)], axis=0).T
    column = lax.rem(lax.broadcasted_iota(i32, columns.shape, 1), requests)
    for k in range(requests):
        own = jnp.where(column == k, columns, 0.0).astype(bf16)
        states[k].wait()
        part = jnp.dot(state_held[k], own, preferred_element_type=f32)
        if k == 0:
            sums[...] = part
        else:
            sums[...] += part
    from_state = sums[...].T

    gate = project(gate_held, gate_parts)
    carried = None
    terms = []
    gated = []
    for slot in range(slots):
        decay, step = of(decays, slot), of(steps, slot)
        current = x[slot].astype(f32)
        carried = decay if carried is None else carried * decay
        terms = [term * decay for term in terms] + [step * current]
        value = carried * of(from_state, slot) + skip * current
        for j, term in enumerate(terms):
            match = jnp.sum(reads[slot] * writes[j], axis=1, keepdims=True)
            value = value + match * term
        gated.append(value * silu(of(gate, slot).astype(f32)))
    gated = jnp.concatenate(gated, axis=0)
    squares = jnp.sum(gated * gated, axis=1, keepdims=True)
    weighted = (gated * gate_gain[...]).astype(bf16)
    depth = weighted.shape[1] // chunks
    total = None
    for c, copy in enumerate(out_parts):
        copy.wait()
        part = jnp.dot(
            weighted[:, c * depth : (c + 1) * depth],
            out_held[pl.ds(c * depth, depth)],
            preferred_element_type=f32,
        )
        total = part if total is None else total + part
    partial_out[...] = total
    wide = jnp.broadcast_to(squares, (rows, 128))
    squares_out[...] = wide
    high = wide.astype(bf16)
    low = (wide - high.astype(f32)).astype(bf16)
    model = total.shape[1]
    packed_out[:, :model] = total.astype(bf16)
    packed_out[:, model : model + 128] = high
    packed_out[:, model + 128 :] = low


def home_tokens(order, tokens, small, big, state, slots, taps):
    rows, model = tokens.shape
    requests, width, state_dim = state.shape
    chunks = 5
    lanes = rows + -rows % 128
    in_vmem = pl.BlockSpec(memory_space=pltpu.VMEM)
    return pl.pallas_call(
        functools.partial(home_body, (requests, slots, state_dim, taps, chunks)),
        grid_spec=pltpu.PrefetchScalarGridSpec(
            num_scalar_prefetch=1,
            grid=(),
            in_specs=[in_vmem] * (1 + len(small)) + [ANY] * (len(big) + 1),
            out_specs=[in_vmem] * 4,
            scratch_shapes=[pltpu.VMEM(w.shape, w.dtype) for w in big]
            + [
                pltpu.VMEM(state.shape, state.dtype),
                pltpu.VMEM((rows, model), bf16),
                pltpu.VMEM((width, lanes), f32),
                pltpu.SemaphoreType.DMA((3 * chunks + 2,)),
                pltpu.SemaphoreType.DMA((requests,)),
            ],
        ),
        out_shape=[
            jax.ShapeDtypeStruct((rows, model + 256), bf16),
            jax.ShapeDtypeStruct((rows, model), f32),
            jax.ShapeDtypeStruct((rows, 128), f32),
            jax.ShapeDtypeStruct((rows, model), bf16),
        ],
        compiler_params=pltpu.CompilerParams(vmem_limit_bytes=48 << 20),
        cost_estimate=pl.CostEstimate(flops=1, bytes_accessed=1, transcendentals=0),
        name="home_tokens",
    )(order, tokens, *small, *big, state)


def update_body(where, heads, target, start, keep, weighted, writes, *refs):
    pieces = refs[: len(where)]
    out, before, after, arrive, leave = refs[-5:]
    steps = [(i, d, first, k) for i, (d, first, size) in enumerate(where) for k in range(size)]
    count = len(steps)

    def at(index):
        _, distance, first, k = steps[index]
        return start[distance] + first + k

    def read(index):
        return pltpu.make_async_copy(
            pieces[steps[index][0]].at[steps[index][3]], before.at[index], arrive.at[index]
        )

    def write(index):
        return pltpu.make_async_copy(after.at[index], out.at[target[at(index)]], leave.at[index])

    for index in range(count):
        read(index).start()
    width = weighted.shape[0] // heads
    for index in range(count):
        request = at(index)
        added = jnp.dot(weighted[...], writes[request], preferred_element_type=f32)
        read(index).wait()
        for head in range(heads):
            rows = slice(head * width, (head + 1) * width)
            after[index, rows] = (
                before[index, rows].astype(f32) * keep[request, head] + added[rows]
            ).astype(bf16)
        write(index).start()
    for index in range(count):
        write(index).wait()


def update_pieces(target, start, keep, weighted, writes, where, pieces, whole):
    width, state_dim = pieces[0].shape[1:]
    req_dev, heads = keep.shape
    where = [(d, first, piece.shape[0]) for (d, first), piece in zip(where, pieces)]
    count = sum(size for _, _, size in where)
    return pl.pallas_call(
        functools.partial(update_body, tuple(where), heads),
        grid_spec=pltpu.PrefetchScalarGridSpec(
            num_scalar_prefetch=3,
            grid=(),
            in_specs=[pl.BlockSpec(memory_space=pltpu.VMEM)] * 2
            + [ANY] * (len(where) + len(whole)),
            out_specs=ANY,
            scratch_shapes=[
                pltpu.VMEM((count, width, state_dim), bf16),
                pltpu.VMEM((count, width, state_dim), bf16),
                pltpu.SemaphoreType.DMA((count,)),
                pltpu.SemaphoreType.DMA((count,)),
            ],
        ),
        out_shape=jax.ShapeDtypeStruct((req_dev, width, state_dim), bf16),
        input_output_aliases={5 + len(where): 0} if whole else {},
        compiler_params=pltpu.CompilerParams(vmem_limit_bytes=24 << 20),
        name="update_pieces",
    )(target, start, keep, weighted, writes, *pieces, *whole)


def head_body(vocab, first, ids, final, rows, top, draft):
    step = pl.program_id(0)
    depth = rows.shape[0]
    logits = lax.dot_general(
        rows[...], final[...], (((1,), (1,)), ((), ())), preferred_element_type=f32
    )
    row = step * depth + lax.broadcasted_iota(i32, logits.shape, 0)
    logits = jnp.where(row < vocab, logits, lowest)
    best = jnp.max(logits, axis=0, keepdims=True)
    match = jnp.max(
        jnp.where(row + first[0] == ids[...], logits, lowest), axis=0, keepdims=True
    )

    @pl.when(step == 0)
    def _():
        top[...] = best
        draft[...] = match

    @pl.when(step > 0)
    def _():
        top[...] = jnp.maximum(top[...], best)
        draft[...] = jnp.maximum(draft[...], match)


def head_logits(first, ids, final, embedding):
    vocab, model = embedding.shape
    tokens = final.shape[0]
    depth = 400
    return pl.pallas_call(
        functools.partial(head_body, vocab),
        grid_spec=pltpu.PrefetchScalarGridSpec(
            num_scalar_prefetch=1,
            grid=(pl.cdiv(vocab, depth),),
            in_specs=[
                pl.BlockSpec((1, tokens), lambda i, first: (0, 0)),
                pl.BlockSpec((tokens, model), lambda i, first: (0, 0)),
                pl.BlockSpec((depth, model), lambda i, first: (i, 0)),
            ],
            out_specs=[pl.BlockSpec((1, tokens), lambda i, first: (0, 0))] * 2,
        ),
        out_shape=[jax.ShapeDtypeStruct((1, tokens), f32)] * 2,
        compiler_params=pltpu.CompilerParams(vmem_limit_bytes=24 << 20),
        cost_estimate=pl.CostEstimate(
            flops=2 * vocab * model * tokens,
            bytes_accessed=2 * vocab * model,
            transcendentals=0,
        ),
        name="head_logits",
    )(first, ids, final, embedding)


def on_device(
    stream_in,
    norm_gain,
    gate_weight,
    inner_weight,
    readwrite_weight,
    step_weight,
    conv_inner,
    conv_readwrite,
    decay_log,
    step_bias,
    skip_gain,
    gate_gain,
    out_weight,
    final_gain,
    embedding,
    state_cache,
    window_inner,
    window_readwrite,
    source_row,
    lengths,
    draft_ids,
):
    n_req = lax.axis_size("req")
    n_head = lax.axis_size("head")
    req_index = lax.axis_index("req")
    head_index = lax.axis_index("head")
    rows_dev, model = stream_in.shape
    req_dev = lengths.shape[0]
    slots = rows_dev // req_dev
    all_req = source_row.shape[0]
    heads_dev, head_width, state_dim = state_cache.shape[1:]
    inner_dev = inner_weight.shape[1]
    vocab_dev = embedding.shape[0]
    share = rows_dev // n_head
    taps = conv_inner.shape[0]

    each = req_dev // n_req
    states = state_cache.reshape(req_dev, inner_dev, state_dim)

    def swap(values, axis, mask):
        return lax.ppermute(values, axis, [(i, i ^ mask) for i in range(lax.axis_size(axis))])

    request = jnp.arange(all_req, dtype=i32)
    block = request // req_dev
    home = source_row // req_dev
    before = (
        (home[None, :] == home[:, None])
        & (block[None, :] == block[:, None])
        & (request[None, :] < request[:, None])
    )
    rank = jnp.sum(before.astype(i32), axis=1)
    place = (block ^ home) * each + rank
    listed = jnp.arange(req_dev, dtype=i32)[:, None]
    is_home = (listed == place[None, :]) & (home == req_index)[None, :]
    is_target = (listed == place[None, :]) & (block == req_index)[None, :]
    start = jnp.arange(n_req, dtype=i32) * each
    home_row = jnp.sum(jnp.where(is_home, (source_row % req_dev)[None, :], 0), axis=1)
    target = jnp.sum(jnp.where(is_target, (request % req_dev)[None, :], 0), axis=1)

    mine = jnp.arange(req_dev, dtype=i32)
    to_target = (target[:, None] == mine[None, :]).astype(bf16)
    to_home = (home_row[:, None] == mine[None, :]).astype(bf16)
    row = jnp.arange(rows_dev, dtype=i32)
    source_token = jnp.repeat(target, slots) * slots + row % slots
    tokens_out = jnp.dot(
        (source_token[:, None] == row[None, :]).astype(bf16),
        stream_in,
        preferred_element_type=f32,
    ).astype(bf16)

    def choose(selector, values):
        return jnp.einsum("kr,rjc->jkc", selector, values, preferred_element_type=f32).astype(bf16)

    home_inner = choose(to_home, window_inner)
    home_readwrite = choose(to_home, window_readwrite)
    lag = taps - 1
    packed_inner = home_inner.reshape(lag, n_req, each * inner_dev).transpose(1, 0, 2)
    packed_readwrite = (
        home_readwrite.reshape(lag, n_req, each * 2 * state_dim)
        .transpose(1, 0, 2)
        .reshape(n_req, 1, lag * each * 2 * state_dim)
    )
    letters = jnp.concatenate(
        [
            tokens_out.reshape(n_req, each * slots, model),
            jnp.pad(packed_inner, ((0, 0), (0, 0), (0, model - packed_inner.shape[2]))),
            jnp.pad(packed_readwrite, ((0, 0), (0, 0), (0, model - packed_readwrite.shape[2]))),
        ],
        axis=1,
    )
    outgoing = letters
    pairs = [letters[:2]]
    for mask in range(2, n_req, 2):
        pairs.append(swap(letters[mask : mask + 2], "req", mask))
    direct = [d for d in range(1, n_req) if d > 3] if n_req > 3 else []
    phases = ([n_req - 2], [d for d in direct if d != n_req - 2])
    home_row_a, outgoing = lax.optimization_barrier((home_row, outgoing))
    pair, *leaving_a = take_pieces(
        home_row_a, start, states, [(2, 3)] + [(d,) for d in phases[0]], each
    )
    pairs, pair, leaving_a = lax.optimization_barrier((pairs, pair, leaving_a))
    arrived = {}
    for d, value in zip(phases[0], leaving_a):
        arrived[d] = swap(value, "req", d)
    pair = swap(pair, "req", 2)
    arrived[2] = pair[:each]
    kept = jnp.stack([both[0] for both in pairs])
    passed = swap(jnp.stack([both[1] for both in pairs]), "req", 1)
    letters = jnp.stack([kept, passed], axis=1).reshape(letters.shape)

    home_stream = letters[:, : each * slots].reshape(rows_dev, model)
    got_inner = (
        letters[:, each * slots : each * slots + lag, : each * inner_dev]
        .transpose(1, 0, 2)
        .reshape(lag, req_dev, inner_dev)
    )
    got_readwrite = (
        letters[:, each * slots + lag, : lag * each * 2 * state_dim]
        .reshape(n_req, lag, each * 2 * state_dim)
        .transpose(1, 0, 2)
        .reshape(lag, req_dev, 2 * state_dim)
    )

    def project(stream):
        stream = stream.astype(f32)
        normed = (stream / rms_of(stream) * norm_gain).astype(bf16)
        inner = jnp.dot(normed, inner_weight, preferred_element_type=f32).astype(bf16)
        readwrite = jnp.dot(normed, readwrite_weight, preferred_element_type=f32).astype(bf16)
        step_raw = jnp.dot(normed, step_weight, preferred_element_type=f32).astype(bf16)
        return normed, inner, readwrite, step_raw

    def windows(old, new):
        new = new.reshape(req_dev, slots, new.shape[1])
        return [old[j] for j in range(lag)] + [new[:, s] for s in range(slots)]

    def conv_silu(rows, weight):
        outs = []
        for slot in range(slots):
            total = jnp.zeros(rows[0].shape, f32)
            for tap in range(taps):
                total = total + rows[slot + tap].astype(f32) * weight[tap].astype(f32)
            outs.append(jax.nn.silu(total).astype(bf16))
        return outs

    def step_sizes(step_raw, live):
        raw = step_raw.astype(f32).reshape(req_dev, slots, heads_dev)
        steps = jax.nn.softplus(raw + step_bias) * live[:, :, None]
        return steps, jnp.exp(-jnp.exp(decay_log) * steps)

    spread = (
        jnp.arange(inner_dev, dtype=i32)[None, :] // head_width
        == jnp.arange(heads_dev, dtype=i32)[:, None]
    ).astype(f32)

    def expand(values):
        return jnp.dot(values, spread, precision=lax.Precision.HIGHEST)

    head_values = jnp.repeat(
        jnp.stack([step_bias, jnp.exp(decay_log), skip_gain]), head_width, axis=1
    )
    packed, partial, squares, home_stream = home_tokens(
        home_row,
        home_stream,
        (
            norm_gain[None, :],
            home_inner,
            home_readwrite,
            conv_inner,
            conv_readwrite,
            spread.astype(bf16),
            head_values,
            gate_gain[None, :],
        ),
        (inner_weight, readwrite_weight, step_weight, gate_weight, out_weight),
        states,
        slots,
        taps,
    )

    def rows_of(values, index):
        return lax.dynamic_slice_in_dim(values, index * share, share)

    mixed = rows_of(partial, head_index)
    total = rows_of(squares, head_index)[:, :1]
    for mask in range(1, n_head):
        part = swap(rows_of(packed, head_index ^ mask), "head", mask).astype(f32)
        mixed = mixed + part[:, :model]
        total = total + part[:, model : model + 1] + part[:, model + 128 : model + 129]
    mixed = mixed / jnp.sqrt(total / (inner_dev * n_head) + epsilon)
    residual = rows_of(home_stream, head_index).astype(f32) + mixed
    scale = rms_of(residual)
    final = (residual / scale * final_gain).astype(bf16)

    distance = [0]
    final, home_row_b = lax.optimization_barrier((final, home_row))
    local, neighbour, *leaving_b = take_pieces(
        home_row_b, start, states, [(0,), (1,)] + [(d,) for d in phases[1]], each
    )
    arrived[0] = local
    for d, value in zip(phases[1][:1], leaving_b):
        arrived[d] = swap(value, "req", d)
    everyone = final
    for step, (axis, masks) in enumerate((
        ("req", range(2, n_req, 2)),
        ("req", (1,)),
        ("head", range(2, n_head, 2)),
        ("head", (1,)),
    )):
        if step == 3:
            first_late = phases[1][0]
            everyone, arrived[first_late] = lax.optimization_barrier(
                (everyone, arrived[first_late])
            )
        everyone = jnp.concatenate([everyone] + [swap(everyone, axis, m) for m in masks], axis=0)
        if step == 1:
            passed_on = jnp.concatenate([neighbour, pair[each:]])
            everyone, passed_on = lax.optimization_barrier((everyone, passed_on))
            passed_on = swap(passed_on, "req", 1)
            arrived[1], arrived[3] = passed_on[:each], passed_on[each:]
        if step in (1, 2):
            some = slice(1, 2) if step == 1 else slice(2, None)
            everyone, *going = lax.optimization_barrier((everyone, *leaving_b[some]))
            for d, value in zip(phases[1][some], going):
                cuts = (0, each) if step == 1 or each == 1 else (0, each // 2, each)
                parts = [swap(value[i:j], "req", d) for i, j in zip(cuts, cuts[1:])]
                arrived[d] = list(zip(cuts, parts)) if step == 2 else parts[0]
        unit = n_head if axis == "req" else 1
        distance = distance + [e ^ (m * unit) for m in masks for e in distance]

    tokens = n_req * rows_dev
    my_req = share // slots
    my_device = req_index * n_head + head_index
    local = jnp.arange(slots, dtype=i32)[None, :] * req_dev + place[:, None]
    local = local.reshape(tokens)
    from_device = jnp.repeat(home, slots) * n_head + local // share
    away = (from_device ^ my_device)[:, None] == jnp.array(distance, dtype=i32)[None, :]
    found_at = jnp.sum(
        jnp.where(away, jnp.arange(len(distance), dtype=i32)[None, :], 0), axis=1
    ) * share + local % share
    token = jnp.arange(tokens, dtype=i32)
    pick = found_at[:, None] == token[None, :]
    ids_here = jnp.sum(jnp.where(pick, draft_ids[:, None], 0), axis=0)
    first_row = jnp.full((1,), my_device * vocab_dev, i32)
    top, draft = head_logits(first_row, ids_here[None, :], everyone, embedding)
    held = [1, 3]
    top, draft, *values = lax.optimization_barrier((top, draft, *(arrived[d] for d in held)))
    arrived.update(zip(held, values))
    scales = jnp.concatenate([scale[:, 0], jnp.full((tokens - share,), lowest, f32)])
    found = jnp.concatenate([top, draft, scales[None, :]])
    found = jnp.max(jnp.where(pick[None], found[:, None, :], lowest), axis=2)
    found = found.reshape(3, n_req, n_head, share)

    def for_head(index):
        return lax.dynamic_index_in_dim(found, index, axis=2, keepdims=False)

    best = for_head(head_index)
    for mask in range(1, n_head):
        best = jnp.maximum(best, swap(for_head(head_index ^ mask), "head", mask))


    def for_req(distance):
        return lax.dynamic_index_in_dim(best, req_index ^ distance, axis=1, keepdims=False)

    far = swap(jnp.stack([for_req(mask ^ 1) for mask in range(0, n_req, 2)]), "req", 1)
    for d in phases[1][2:]:
        first, part = arrived[d][0]
        far, part = lax.optimization_barrier((far, part))
        arrived[d][0] = (first, part)
    for d in phases[1][1:2]:
        far, arrived[d] = lax.optimization_barrier((far, arrived[d]))
    own = jnp.maximum(for_req(0), far[0])
    for mask in range(2, n_req, 2):
        own = jnp.maximum(own, swap(jnp.maximum(for_req(mask), far[mask // 2]), "req", mask))
    my_lengths = lax.dynamic_slice_in_dim(lengths, head_index * my_req, my_req)
    live = jnp.arange(slots, dtype=i32)[None, :] < my_lengths[:, None]
    own = jnp.where(live.reshape(1, share), own, 0.0)

    tokens_out, got_inner, got_readwrite, _ = lax.optimization_barrier(
        (tokens_out, got_inner, got_readwrite, final)
    )
    _, inner, readwrite, step_raw = project(tokens_out)
    rows_inner = windows(got_inner, inner)
    rows_readwrite = windows(got_readwrite, readwrite)
    my_lengths = jnp.sum(jnp.where(to_target > 0, lengths[None, :], 0), axis=1)

    def tails(rows):
        picked = []
        for j in range(lag):
            value = rows[j + 1]
            for length in range(2, slots + 1):
                value = jnp.where(my_lengths[:, None] == length, rows[j + length], value)
            picked.append(value)
        picked = jnp.stack(picked, axis=1)
        return jnp.einsum("kr,kjc->rjc", to_target, picked, preferred_element_type=f32).astype(bf16)

    tail_inner = tails(rows_inner)
    tail_readwrite = tails(rows_readwrite)
    conv_x = conv_silu(rows_inner, conv_inner)
    writes = jnp.stack(conv_silu(rows_readwrite, conv_readwrite), axis=1)[..., :state_dim]
    live = (jnp.arange(slots, dtype=i32)[None, :] < my_lengths[:, None]).astype(f32)
    steps, decays = step_sizes(step_raw, live)
    keep = jnp.ones((req_dev, heads_dev), f32)
    terms = []
    for slot in reversed(range(slots)):
        terms.append(keep * steps[:, slot])
        keep = keep * decays[:, slot]
    wide = expand(jnp.concatenate(terms[::-1], axis=0)).reshape(slots, req_dev, inner_dev)
    weighted = jnp.stack([wide[s] * conv_x[s].astype(f32) for s in range(slots)], axis=1)
    high = weighted.astype(bf16)
    low = (weighted - high.astype(f32)).astype(bf16)
    count = 2 * slots * req_dev
    weighted = jnp.concatenate([high, low], axis=1).reshape(count, inner_dev).T
    writes = jnp.concatenate([writes, writes], axis=1).reshape(1, count, state_dim)
    owner = jnp.arange(count, dtype=i32)[None, :, None] // (2 * slots)
    writes = jnp.where(owner == mine[:, None, None], writes, 0)

    update = functools.partial(update_pieces, target, start, keep, weighted, writes)
    early = [0, 1, 2, 3] + phases[0] + phases[1][:2]
    after = update([(d, 0) for d in early], [arrived[d] for d in early], ())
    last = phases[1][2:]
    late = [(d, first) for d in last for first, _ in arrived[d]]
    after = update(late, [part for d in last for _, part in arrived[d]], (after,))
    state_after = after.reshape(state_cache.shape)
    top_logit, draft_logit, hidden_rms = own
    return (state_after, tail_inner, tail_readwrite, hidden_rms, top_logit, draft_logit)


def solution(mesh):
    in_specs = (
        P("req", None),
        P(),
        P(None, "head"),
        P(None, "head"),
        P(),
        P(None, "head"),
        P(None, "head"),
        P(),
        P("head"),
        P("head"),
        P("head"),
        P("head"),
        P("head", None),
        P(),
        P(("req", "head"), None),
        P("req", "head", None, None),
        P("req", None, "head"),
        P("req", None, None),
        P(),
        P("req"),
        P(),
    )
    out_specs = (
        P("req", "head", None, None),
        P("req", None, "head"),
        P("req", None, None),
        P(("req", "head")),
        P(("req", "head")),
        P(("req", "head")),
    )
    return jax.shard_map(
        on_device, mesh=mesh, in_specs=in_specs, out_specs=out_specs, check_vma=False
    )
```

```python
import functools

import jax
import jax.numpy as jnp
from jax import lax
from jax.experimental import pallas as pl
from jax.experimental.pallas import tpu as pltpu
from jax.sharding import PartitionSpec as P

epsilon = 1e-05
lowest = -1e30
f32 = jnp.float32
bf16 = jnp.bfloat16
i32 = jnp.int32
ANY = pl.BlockSpec(memory_space=pl.ANY)


def rms_of(values):
    return jnp.sqrt(jnp.mean(values * values, axis=-1, keepdims=True) + epsilon)


def pieces_body(where, size, rows, start, held, *refs):
    outs, (buffer, arrive, leave) = refs[:-3], refs[-3:]
    steps = [
        (distance, k, piece, order * size + k)
        for piece, distances in enumerate(where)
        for order, distance in enumerate(distances)
        for k in range(size)
    ]

    def read(index):
        distance, k = steps[index][:2]
        return pltpu.make_async_copy(
            held.at[rows[start[distance] + k]], buffer.at[index], arrive.at[index]
        )

    def write(index):
        piece, at = steps[index][2:]
        return pltpu.make_async_copy(buffer.at[index], outs[piece].at[at], leave.at[index])

    for index in range(len(steps)):
        read(index).start()
    for index in range(len(steps)):
        read(index).wait()
        write(index).start()
    for index in range(len(steps)):
        write(index).wait()


def take_pieces(rows, start, held, where, size):
    width, depth = held.shape[1:]
    count = size * sum(len(distances) for distances in where)
    return pl.pallas_call(
        functools.partial(pieces_body, tuple(where), size),
        grid_spec=pltpu.PrefetchScalarGridSpec(
            num_scalar_prefetch=2,
            grid=(),
            in_specs=[ANY],
            out_specs=[ANY] * len(where),
            scratch_shapes=[
                pltpu.VMEM((count, width, depth), held.dtype),
                pltpu.SemaphoreType.DMA((count,)),
                pltpu.SemaphoreType.DMA((count,)),
            ],
        ),
        out_shape=[
            jax.ShapeDtypeStruct((size * len(distances), width, depth), held.dtype)
            for distances in where
        ],
        cost_estimate=pl.CostEstimate(flops=1, bytes_accessed=1, transcendentals=0),
        name="take_pieces",
    )(rows, start, held)


def softplus(values):
    return jnp.maximum(values, 0.0) + jnp.log1p(jnp.exp(-jnp.abs(values)))


def silu(values):
    return values / (1.0 + jnp.exp(-values))


def home_body(
    sizes,
    order,
    tokens,
    norm_gain,
    old_inner,
    old_readwrite,
    conv_inner,
    conv_readwrite,
    heads,
    head_values,
    gate_gain,
    weights_inner,
    weights_readwrite,
    weights_step,
    weights_gate,
    weights_out,
    state,
    packed_out,
    partial_out,
    squares_out,
    stream_out,
    inner_held,
    readwrite_held,
    step_held,
    gate_held,
    out_held,
    state_held,
    normed,
    sums,
    sems,
    state_sems,
):
    requests, slots, state_dim, taps, chunks = sizes
    rows = requests * slots
    lag = taps - 1

    def parts(source, held, at):
        depth = source.shape[0] // chunks
        return [
            pltpu.make_async_copy(
                source.at[pl.ds(c * depth, depth)],
                held.at[pl.ds(c * depth, depth)],
                sems.at[at * chunks + c],
            )
            for c in range(chunks)
        ]

    inner_parts = parts(weights_inner, inner_held, 0)
    gate_parts = parts(weights_gate, gate_held, 1)
    out_parts = parts(weights_out, out_held, 2)
    small = [
        pltpu.make_async_copy(weights_readwrite, readwrite_held, sems.at[3 * chunks]),
        pltpu.make_async_copy(weights_step, step_held, sems.at[3 * chunks + 1]),
    ]
    states = [
        pltpu.make_async_copy(state.at[order[k]], state_held.at[k], state_sems.at[k])
        for k in range(requests)
    ]
    for copy in small + inner_parts + states + gate_parts + out_parts:
        copy.start()

    into = lax.broadcasted_iota(i32, (rows, rows), 0)
    origin = lax.broadcasted_iota(i32, (rows, rows), 1)
    by_slot = (origin == lax.rem(into, requests) * slots + lax.div(into, requests)).astype(bf16)
    stream_bf = jnp.dot(by_slot, tokens[...], preferred_element_type=f32)
    stream_out[...] = stream_bf.astype(bf16)
    scale = jnp.sqrt(jnp.mean(stream_bf * stream_bf, axis=1, keepdims=True) + epsilon)
    normed[...] = (stream_bf / scale * norm_gain[...]).astype(bf16)

    def project(held, copies):
        total = None
        depth = held.shape[0] // len(copies)
        for c, copy in enumerate(copies):
            copy.wait()
            span = pl.ds(c * depth, depth)
            part = jnp.dot(normed[:, span], held[span], preferred_element_type=f32)
            total = part if total is None else total + part
        return total.astype(bf16)

    readwrite = project(readwrite_held, small[:1])
    step_raw = project(step_held, small[1:])
    inner = project(inner_held, inner_parts)

    def of(values, slot):
        return values[slot * requests : (slot + 1) * requests]

    def convolve(old, new, weight):
        window = [old[j].astype(f32) for j in range(lag)]
        window = window + [of(new, slot).astype(f32) for slot in range(slots)]
        outs = []
        for slot in range(slots):
            total = None
            for tap in range(taps):
                part = window[slot + tap] * weight[tap : tap + 1].astype(f32)
                total = part if total is None else total + part
            outs.append(silu(total).astype(bf16))
        return outs

    x = convolve(old_inner, inner, conv_inner[...])
    vectors = convolve(old_readwrite, readwrite, conv_readwrite[...])
    writes = [v[:, :state_dim].astype(f32) for v in vectors]
    reads = [v[:, state_dim:].astype(f32) for v in vectors]

    bias, decay_rate, skip = (head_values[i : i + 1] for i in range(3))
    wide_step = jnp.dot(step_raw, heads[...], preferred_element_type=f32)
    steps = softplus(wide_step + bias)
    decays = jnp.exp(-decay_rate * steps)

    columns = jnp.concatenate(reads + [jnp.zeros((sums.shape[1] - rows, state_dim), f32)], axis=0).T
    column = lax.rem(lax.broadcasted_iota(i32, columns.shape, 1), requests)
    for k in range(0, requests, 2):
        both = range(k, min(k + 2, requests))
        own = [jnp.where(column == i, columns, 0.0).astype(bf16) for i in both]
        for i in both:
            states[i].wait()
        part = jnp.dot(
            jnp.concatenate([state_held[i] for i in both], axis=1),
            jnp.concatenate(own, axis=0),
            preferred_element_type=f32,
        )
        if k == 0:
            sums[...] = part
        else:
            sums[...] += part
    from_state = sums[...].T

    gate = project(gate_held, gate_parts)
    carried = None
    terms = []
    gated = []
    for slot in range(slots):
        decay, step = of(decays, slot), of(steps, slot)
        current = x[slot].astype(f32)
        carried = decay if carried is None else carried * decay
        terms = [term * decay for term in terms] + [step * current]
        value = carried * of(from_state, slot) + skip * current
        for j, term in enumerate(terms):
            match = jnp.sum(reads[slot] * writes[j], axis=1, keepdims=True)
            value = value + match * term
        gated.append(value * silu(of(gate, slot).astype(f32)))
    gated = jnp.concatenate(gated, axis=0)
    squares = jnp.sum(gated * gated, axis=1, keepdims=True)
    weighted = (gated * gate_gain[...]).astype(bf16)
    depth = weighted.shape[1] // chunks
    total = None
    for c, copy in enumerate(out_parts):
        copy.wait()
        part = jnp.dot(
            weighted[:, c * depth : (c + 1) * depth],
            out_held[pl.ds(c * depth, depth)],
            preferred_element_type=f32,
        )
        total = part if total is None else total + part
    partial_out[...] = total
    wide = jnp.broadcast_to(squares, (rows, 128))
    squares_out[...] = wide
    high = wide.astype(bf16)
    low = (wide - high.astype(f32)).astype(bf16)
    model = total.shape[1]
    packed_out[:, :model] = total.astype(bf16)
    packed_out[:, model : model + 128] = high
    packed_out[:, model + 128 :] = low


def home_tokens(order, tokens, small, big, state, slots, taps):
    rows, model = tokens.shape
    requests, width, state_dim = state.shape
    chunks = 5
    lanes = rows + -rows % 128
    in_vmem = pl.BlockSpec(memory_space=pltpu.VMEM)
    return pl.pallas_call(
        functools.partial(home_body, (requests, slots, state_dim, taps, chunks)),
        grid_spec=pltpu.PrefetchScalarGridSpec(
            num_scalar_prefetch=1,
            grid=(),
            in_specs=[in_vmem] * (1 + len(small)) + [ANY] * (len(big) + 1),
            out_specs=[in_vmem] * 4,
            scratch_shapes=[pltpu.VMEM(w.shape, w.dtype) for w in big]
            + [
                pltpu.VMEM(state.shape, state.dtype),
                pltpu.VMEM((rows, model), bf16),
                pltpu.VMEM((width, lanes), f32),
                pltpu.SemaphoreType.DMA((3 * chunks + 2,)),
                pltpu.SemaphoreType.DMA((requests,)),
            ],
        ),
        out_shape=[
            jax.ShapeDtypeStruct((rows, model + 256), bf16),
            jax.ShapeDtypeStruct((rows, model), f32),
            jax.ShapeDtypeStruct((rows, 128), f32),
            jax.ShapeDtypeStruct((rows, model), bf16),
        ],
        compiler_params=pltpu.CompilerParams(vmem_limit_bytes=48 << 20),
        cost_estimate=pl.CostEstimate(flops=1, bytes_accessed=1, transcendentals=0),
        name="home_tokens",
    )(order, tokens, *small, *big, state)


def update_body(where, heads, target, start, keep, weighted, writes, *refs):
    pieces = refs[: len(where)]
    out, before, after, arrive, leave = refs[-5:]
    steps = [(i, d, first, k) for i, (d, first, size) in enumerate(where) for k in range(size)]
    count = len(steps)

    def at(index):
        _, distance, first, k = steps[index]
        return start[distance] + first + k

    def read(index):
        return pltpu.make_async_copy(
            pieces[steps[index][0]].at[steps[index][3]], before.at[index], arrive.at[index]
        )

    def write(index):
        return pltpu.make_async_copy(after.at[index], out.at[target[at(index)]], leave.at[index])

    for index in range(count):
        read(index).start()
    width = weighted.shape[0] // heads
    for index in range(count):
        request = at(index)
        added = jnp.dot(weighted[...], writes[request], preferred_element_type=f32)
        read(index).wait()
        for head in range(heads):
            rows = slice(head * width, (head + 1) * width)
            after[index, rows] = (
                before[index, rows].astype(f32) * keep[request, head] + added[rows]
            ).astype(bf16)
        write(index).start()
    for index in range(count):
        write(index).wait()


def update_pieces(target, start, keep, weighted, writes, where, pieces, whole):
    width, state_dim = pieces[0].shape[1:]
    req_dev, heads = keep.shape
    where = [(d, first, piece.shape[0]) for (d, first), piece in zip(where, pieces)]
    count = sum(size for _, _, size in where)
    return pl.pallas_call(
        functools.partial(update_body, tuple(where), heads),
        grid_spec=pltpu.PrefetchScalarGridSpec(
            num_scalar_prefetch=3,
            grid=(),
            in_specs=[pl.BlockSpec(memory_space=pltpu.VMEM)] * 2
            + [ANY] * (len(where) + len(whole)),
            out_specs=ANY,
            scratch_shapes=[
                pltpu.VMEM((count, width, state_dim), bf16),
                pltpu.VMEM((count, width, state_dim), bf16),
                pltpu.SemaphoreType.DMA((count,)),
                pltpu.SemaphoreType.DMA((count,)),
            ],
        ),
        out_shape=jax.ShapeDtypeStruct((req_dev, width, state_dim), bf16),
        input_output_aliases={5 + len(where): 0} if whole else {},
        compiler_params=pltpu.CompilerParams(vmem_limit_bytes=24 << 20),
        name="update_pieces",
    )(target, start, keep, weighted, writes, *pieces, *whole)


def head_body(vocab, first, ids, final, rows, top, draft):
    step = pl.program_id(0)
    depth = rows.shape[0]
    logits = lax.dot_general(
        rows[...], final[...], (((1,), (1,)), ((), ())), preferred_element_type=f32
    )
    row = step * depth + lax.broadcasted_iota(i32, logits.shape, 0)
    logits = jnp.where(row < vocab, logits, lowest)
    best = jnp.max(logits, axis=0, keepdims=True)
    match = jnp.max(
        jnp.where(row + first[0] == ids[...], logits, lowest), axis=0, keepdims=True
    )

    @pl.when(step == 0)
    def _():
        top[...] = best
        draft[...] = match

    @pl.when(step > 0)
    def _():
        top[...] = jnp.maximum(top[...], best)
        draft[...] = jnp.maximum(draft[...], match)


def head_logits(first, ids, final, embedding):
    vocab, model = embedding.shape
    tokens = final.shape[0]
    depth = 400
    return pl.pallas_call(
        functools.partial(head_body, vocab),
        grid_spec=pltpu.PrefetchScalarGridSpec(
            num_scalar_prefetch=1,
            grid=(pl.cdiv(vocab, depth),),
            in_specs=[
                pl.BlockSpec((1, tokens), lambda i, first: (0, 0)),
                pl.BlockSpec((tokens, model), lambda i, first: (0, 0)),
                pl.BlockSpec((depth, model), lambda i, first: (i, 0)),
            ],
            out_specs=[pl.BlockSpec((1, tokens), lambda i, first: (0, 0))] * 2,
        ),
        out_shape=[jax.ShapeDtypeStruct((1, tokens), f32)] * 2,
        compiler_params=pltpu.CompilerParams(vmem_limit_bytes=24 << 20),
        cost_estimate=pl.CostEstimate(
            flops=2 * vocab * model * tokens,
            bytes_accessed=2 * vocab * model,
            transcendentals=0,
        ),
        name="head_logits",
    )(first, ids, final, embedding)


def on_device(
    stream_in,
    norm_gain,
    gate_weight,
    inner_weight,
    readwrite_weight,
    step_weight,
    conv_inner,
    conv_readwrite,
    decay_log,
    step_bias,
    skip_gain,
    gate_gain,
    out_weight,
    final_gain,
    embedding,
    state_cache,
    window_inner,
    window_readwrite,
    source_row,
    lengths,
    draft_ids,
):
    n_req = lax.axis_size("req")
    n_head = lax.axis_size("head")
    req_index = lax.axis_index("req")
    head_index = lax.axis_index("head")
    rows_dev, model = stream_in.shape
    req_dev = lengths.shape[0]
    slots = rows_dev // req_dev
    all_req = source_row.shape[0]
    heads_dev, head_width, state_dim = state_cache.shape[1:]
    inner_dev = inner_weight.shape[1]
    vocab_dev = embedding.shape[0]
    share = rows_dev // n_head
    taps = conv_inner.shape[0]

    each = req_dev // n_req
    states = state_cache.reshape(req_dev, inner_dev, state_dim)

    def swap(values, axis, mask):
        return lax.ppermute(values, axis, [(i, i ^ mask) for i in range(lax.axis_size(axis))])

    request = jnp.arange(all_req, dtype=i32)
    block = request // req_dev
    home = source_row // req_dev
    before = (
        (home[None, :] == home[:, None])
        & (block[None, :] == block[:, None])
        & (request[None, :] < request[:, None])
    )
    rank = jnp.sum(before.astype(i32), axis=1)
    place = (block ^ home) * each + rank
    listed = jnp.arange(req_dev, dtype=i32)[:, None]
    is_home = (listed == place[None, :]) & (home == req_index)[None, :]
    is_target = (listed == place[None, :]) & (block == req_index)[None, :]
    start = jnp.arange(n_req, dtype=i32) * each
    home_row = jnp.sum(jnp.where(is_home, (source_row % req_dev)[None, :], 0), axis=1)
    target = jnp.sum(jnp.where(is_target, (request % req_dev)[None, :], 0), axis=1)

    mine = jnp.arange(req_dev, dtype=i32)
    to_target = (target[:, None] == mine[None, :]).astype(bf16)
    to_home = (home_row[:, None] == mine[None, :]).astype(bf16)
    row = jnp.arange(rows_dev, dtype=i32)
    source_token = jnp.repeat(target, slots) * slots + row % slots
    tokens_out = jnp.dot(
        (source_token[:, None] == row[None, :]).astype(bf16),
        stream_in,
        preferred_element_type=f32,
    ).astype(bf16)

    def choose(selector, values):
        return jnp.einsum("kr,rjc->jkc", selector, values, preferred_element_type=f32).astype(bf16)

    home_inner = choose(to_home, window_inner)
    home_readwrite = choose(to_home, window_readwrite)
    lag = taps - 1
    packed_inner = home_inner.reshape(lag, n_req, each * inner_dev).transpose(1, 0, 2)
    packed_readwrite = (
        home_readwrite.reshape(lag, n_req, each * 2 * state_dim)
        .transpose(1, 0, 2)
        .reshape(n_req, 1, lag * each * 2 * state_dim)
    )
    letters = jnp.concatenate(
        [
            tokens_out.reshape(n_req, each * slots, model),
            jnp.pad(packed_inner, ((0, 0), (0, 0), (0, model - packed_inner.shape[2]))),
            jnp.pad(packed_readwrite, ((0, 0), (0, 0), (0, model - packed_readwrite.shape[2]))),
        ],
        axis=1,
    )
    outgoing = letters
    pairs = [letters[:2]]
    for mask in range(2, n_req, 2):
        pairs.append(swap(letters[mask : mask + 2], "req", mask))
    direct = [d for d in range(1, n_req) if d > 3] if n_req > 3 else []
    phases = ([n_req - 2], [d for d in direct if d != n_req - 2])
    home_row_a, outgoing = lax.optimization_barrier((home_row, outgoing))
    pair, *leaving_a = take_pieces(
        home_row_a, start, states, [(2, 3)] + [(d,) for d in phases[0]], each
    )
    pairs, pair, leaving_a = lax.optimization_barrier((pairs, pair, leaving_a))
    arrived = {}
    for d, value in zip(phases[0], leaving_a):
        arrived[d] = swap(value, "req", d)
    pair = swap(pair, "req", 2)
    arrived[2] = pair[:each]
    kept = jnp.stack([both[0] for both in pairs])
    passed = swap(jnp.stack([both[1] for both in pairs]), "req", 1)
    letters = jnp.stack([kept, passed], axis=1).reshape(letters.shape)

    home_stream = letters[:, : each * slots].reshape(rows_dev, model)
    got_inner = (
        letters[:, each * slots : each * slots + lag, : each * inner_dev]
        .transpose(1, 0, 2)
        .reshape(lag, req_dev, inner_dev)
    )
    got_readwrite = (
        letters[:, each * slots + lag, : lag * each * 2 * state_dim]
        .reshape(n_req, lag, each * 2 * state_dim)
        .transpose(1, 0, 2)
        .reshape(lag, req_dev, 2 * state_dim)
    )

    def project(stream):
        stream = stream.astype(f32)
        normed = (stream / rms_of(stream) * norm_gain).astype(bf16)
        inner = jnp.dot(normed, inner_weight, preferred_element_type=f32).astype(bf16)
        readwrite = jnp.dot(normed, readwrite_weight, preferred_element_type=f32).astype(bf16)
        step_raw = jnp.dot(normed, step_weight, preferred_element_type=f32).astype(bf16)
        return normed, inner, readwrite, step_raw

    def windows(old, new):
        new = new.reshape(req_dev, slots, new.shape[1])
        return [old[j] for j in range(lag)] + [new[:, s] for s in range(slots)]

    def conv_silu(rows, weight):
        outs = []
        for slot in range(slots):
            total = jnp.zeros(rows[0].shape, f32)
            for tap in range(taps):
                total = total + rows[slot + tap].astype(f32) * weight[tap].astype(f32)
            outs.append(jax.nn.silu(total).astype(bf16))
        return outs

    def step_sizes(step_raw, live):
        raw = step_raw.astype(f32).reshape(req_dev, slots, heads_dev)
        steps = jax.nn.softplus(raw + step_bias) * live[:, :, None]
        return steps, jnp.exp(-jnp.exp(decay_log) * steps)

    spread = (
        jnp.arange(inner_dev, dtype=i32)[None, :] // head_width
        == jnp.arange(heads_dev, dtype=i32)[:, None]
    ).astype(f32)

    def expand(values):
        return jnp.dot(values, spread, precision=lax.Precision.HIGHEST)

    head_values = jnp.repeat(
        jnp.stack([step_bias, jnp.exp(decay_log), skip_gain]), head_width, axis=1
    )
    packed, partial, squares, home_stream = home_tokens(
        home_row,
        home_stream,
        (
            norm_gain[None, :],
            home_inner,
            home_readwrite,
            conv_inner,
            conv_readwrite,
            spread.astype(bf16),
            head_values,
            gate_gain[None, :],
        ),
        (inner_weight, readwrite_weight, step_weight, gate_weight, out_weight),
        states,
        slots,
        taps,
    )

    def rows_of(values, index):
        return lax.dynamic_slice_in_dim(values, index * share, share)

    mixed = rows_of(partial, head_index)
    total = rows_of(squares, head_index)[:, :1]
    for mask in range(1, n_head):
        part = swap(rows_of(packed, head_index ^ mask), "head", mask).astype(f32)
        mixed = mixed + part[:, :model]
        total = total + part[:, model : model + 1] + part[:, model + 128 : model + 129]
    mixed = mixed / jnp.sqrt(total / (inner_dev * n_head) + epsilon)
    residual = rows_of(home_stream, head_index).astype(f32) + mixed
    scale = rms_of(residual)
    final = (residual / scale * final_gain).astype(bf16)

    distance = [0]
    final, home_row_b = lax.optimization_barrier((final, home_row))
    local, neighbour, *leaving_b = take_pieces(
        home_row_b, start, states, [(0,), (1,)] + [(d,) for d in phases[1]], each
    )
    arrived[0] = local
    for d, value in zip(phases[1][:1], leaving_b):
        arrived[d] = swap(value, "req", d)
    everyone = final
    for step, (axis, masks) in enumerate((
        ("req", range(2, n_req, 2)),
        ("req", (1,)),
        ("head", range(2, n_head, 2)),
        ("head", (1,)),
    )):
        if step == 3:
            first_late = phases[1][0]
            everyone, arrived[first_late] = lax.optimization_barrier(
                (everyone, arrived[first_late])
            )
        everyone = jnp.concatenate([everyone] + [swap(everyone, axis, m) for m in masks], axis=0)
        if step == 1:
            passed_on = jnp.concatenate([neighbour, pair[each:]])
            everyone, passed_on = lax.optimization_barrier((everyone, passed_on))
            passed_on = swap(passed_on, "req", 1)
            arrived[1], arrived[3] = passed_on[:each], passed_on[each:]
        if step in (1, 2):
            some = slice(1, 2) if step == 1 else slice(2, None)
            everyone, *going = lax.optimization_barrier((everyone, *leaving_b[some]))
            for d, value in zip(phases[1][some], going):
                cuts = (0, each) if step == 1 or each == 1 else (0, each // 2, each)
                parts = [swap(value[i:j], "req", d) for i, j in zip(cuts, cuts[1:])]
                arrived[d] = list(zip(cuts, parts)) if step == 2 else parts[0]
        unit = n_head if axis == "req" else 1
        distance = distance + [e ^ (m * unit) for m in masks for e in distance]

    tokens = n_req * rows_dev
    my_req = share // slots
    my_device = req_index * n_head + head_index
    local = jnp.arange(slots, dtype=i32)[None, :] * req_dev + place[:, None]
    local = local.reshape(tokens)
    from_device = jnp.repeat(home, slots) * n_head + local // share
    away = (from_device ^ my_device)[:, None] == jnp.array(distance, dtype=i32)[None, :]
    found_at = jnp.sum(
        jnp.where(away, jnp.arange(len(distance), dtype=i32)[None, :], 0), axis=1
    ) * share + local % share
    token = jnp.arange(tokens, dtype=i32)
    pick = found_at[:, None] == token[None, :]
    ids_here = jnp.sum(jnp.where(pick, draft_ids[:, None], 0), axis=0)
    first_row = jnp.full((1,), my_device * vocab_dev, i32)
    top, draft = head_logits(first_row, ids_here[None, :], everyone, embedding)
    held = [1, 3]
    top, draft, *values = lax.optimization_barrier((top, draft, *(arrived[d] for d in held)))
    arrived.update(zip(held, values))
    scales = jnp.concatenate([scale[:, 0], jnp.full((tokens - share,), lowest, f32)])
    found = jnp.concatenate([top, draft, scales[None, :]])
    found = jnp.max(jnp.where(pick[None], found[:, None, :], lowest), axis=2)
    found = found.reshape(3, n_req, n_head, share)

    def for_head(index):
        return lax.dynamic_index_in_dim(found, index, axis=2, keepdims=False)

    best = for_head(head_index)
    for mask in range(1, n_head):
        best = jnp.maximum(best, swap(for_head(head_index ^ mask), "head", mask))


    def for_req(distance):
        return lax.dynamic_index_in_dim(best, req_index ^ distance, axis=1, keepdims=False)

    far = swap(jnp.stack([for_req(mask ^ 1) for mask in range(0, n_req, 2)]), "req", 1)
    for d in phases[1][2:]:
        first, part = arrived[d][0]
        far, part = lax.optimization_barrier((far, part))
        arrived[d][0] = (first, part)
    for d in phases[1][1:2]:
        far, arrived[d] = lax.optimization_barrier((far, arrived[d]))
    own = jnp.maximum(for_req(0), far[0])
    for mask in range(2, n_req, 2):
        own = jnp.maximum(own, swap(jnp.maximum(for_req(mask), far[mask // 2]), "req", mask))
    my_lengths = lax.dynamic_slice_in_dim(lengths, head_index * my_req, my_req)
    live = jnp.arange(slots, dtype=i32)[None, :] < my_lengths[:, None]
    own = jnp.where(live.reshape(1, share), own, 0.0)

    tokens_out, got_inner, got_readwrite, _ = lax.optimization_barrier(
        (tokens_out, got_inner, got_readwrite, final)
    )
    _, inner, readwrite, step_raw = project(tokens_out)
    rows_inner = windows(got_inner, inner)
    rows_readwrite = windows(got_readwrite, readwrite)
    my_lengths = jnp.sum(jnp.where(to_target > 0, lengths[None, :], 0), axis=1)

    def tails(rows):
        picked = []
        for j in range(lag):
            value = rows[j + 1]
            for length in range(2, slots + 1):
                value = jnp.where(my_lengths[:, None] == length, rows[j + length], value)
            picked.append(value)
        picked = jnp.stack(picked, axis=1)
        return jnp.einsum("kr,kjc->rjc", to_target, picked, preferred_element_type=f32).astype(bf16)

    tail_inner = tails(rows_inner)
    tail_readwrite = tails(rows_readwrite)
    conv_x = conv_silu(rows_inner, conv_inner)
    writes = jnp.stack(conv_silu(rows_readwrite, conv_readwrite), axis=1)[..., :state_dim]
    live = (jnp.arange(slots, dtype=i32)[None, :] < my_lengths[:, None]).astype(f32)
    steps, decays = step_sizes(step_raw, live)
    keep = jnp.ones((req_dev, heads_dev), f32)
    terms = []
    for slot in reversed(range(slots)):
        terms.append(keep * steps[:, slot])
        keep = keep * decays[:, slot]
    wide = expand(jnp.concatenate(terms[::-1], axis=0)).reshape(slots, req_dev, inner_dev)
    weighted = jnp.stack([wide[s] * conv_x[s].astype(f32) for s in range(slots)], axis=1)
    high = weighted.astype(bf16)
    low = (weighted - high.astype(f32)).astype(bf16)
    count = 2 * slots * req_dev
    weighted = jnp.concatenate([high, low], axis=1).reshape(count, inner_dev).T
    writes = jnp.concatenate([writes, writes], axis=1).reshape(1, count, state_dim)
    owner = jnp.arange(count, dtype=i32)[None, :, None] // (2 * slots)
    writes = jnp.where(owner == mine[:, None, None], writes, 0)

    update = functools.partial(update_pieces, target, start, keep, weighted, writes)
    early = [0, 1, 2, 3] + phases[0] + phases[1][:2]
    after = update([(d, 0) for d in early], [arrived[d] for d in early], ())
    last = phases[1][2:]
    late = [(d, first) for d in last for first, _ in arrived[d]]
    after = update(late, [part for d in last for _, part in arrived[d]], (after,))
    state_after = after.reshape(state_cache.shape)
    top_logit, draft_logit, hidden_rms = own
    return (state_after, tail_inner, tail_readwrite, hidden_rms, top_logit, draft_logit)


def solution(mesh):
    in_specs = (
        P("req", None),
        P(),
        P(None, "head"),
        P(None, "head"),
        P(),
        P(None, "head"),
        P(None, "head"),
        P(),
        P("head"),
        P("head"),
        P("head"),
        P("head"),
        P("head", None),
        P(),
        P(("req", "head"), None),
        P("req", "head", None, None),
        P("req", None, "head"),
        P("req", None, None),
        P(),
        P("req"),
        P(),
    )
    out_specs = (
        P("req", "head", None, None),
        P("req", None, "head"),
        P("req", None, None),
        P(("req", "head")),
        P(("req", "head")),
        P(("req", "head")),
    )
    return jax.shard_map(
        on_device, mesh=mesh, in_specs=in_specs, out_specs=out_specs, check_vma=False
    )
```
